32 devices in a mesh: ha: 4 (over z), wa: 2 (over y), ba: 4 (over x, core).
Axes of the slice: x: 2, y: 2, z: 4, core: 2. Of those that a mesh axis runs over, the one named last changes fastest.
Arguments:
- tokens: bfloat16 [32, 32, 16, 512], P('ba', 'ha', 'wa'), parts along dimension 0, may hold values from -6 to 6
- norm_gain: float32 [3, 512], replicated, may hold values from 0.1 to 1.9
- w_gatevals: bfloat16 [3, 512, 2048], replicated, may hold values from -0.25 to 0.25
- w_coupling: bfloat16 [3, 512, 128], replicated, may hold values from -0.25 to 0.25
- w_steps: bfloat16 [3, 512, 16], replicated, may hold values from -0.25 to 0.25
- conv_values: float32 [3, 4, 1024], replicated, may hold values from -3 to 3
- conv_coupling: float32 [3, 4, 128], replicated, may hold values from -3 to 3
- step_bias: float32 [3, 16], replicated, may hold values from -4 to 0
- rate_log: float32 [3, 16], replicated, may hold values from -1.5 to 1.5
- skip_gain: float32 [3, 16], replicated, may hold values from 0.5 to 2
- out_gain: float32 [3, 1024], replicated, may hold values from 0.1 to 1.9
- w_output: bfloat16 [3, 1024, 512], replicated, may hold values from -0.1875 to 0.1875
Outputs:
- result: bfloat16 [32, 32, 16, 512], P('ba', 'ha', 'wa'), parts along dimension 0
The draws below stay inside these ranges and needn't reach their ends.
There are 4 independent parts, one for each index of `ba`. The reference program is written for one: setup_inputs(seed, part) draws one part's arguments, and reference() takes and returns one part's arrays. A program takes and returns all parts, laid end to end along the dimension named above; an argument that names none is the same for every part. Nothing has to cross between parts.
All inputs are finite; a program needn't handle non-finite values.
Results may differ from the reference program's by a relative error of at most 0.025.
Values may be sent and summed in bfloat16 or wider, within the bound.
A program may use at most 128 MiB of HBM per device.

```python
import math
import jax
import jax.numpy as jnp
from jax import lax

D = 512
INNER = 1024
STATE = 64
CONV = 4
LAYERS = 3
FRAMES = 8
HEADS = 16
HEIGHT = 32
WIDTH = 16


def shard_levels(stream_key, dims, shards, smallest, largest):
    def one(dim, shards_of):
        draws = jax.random.uniform(jax.random.fold_in(jax.random.fold_in(stream_key, 6), dim), (shards_of,), jnp.float32, smallest / len(shards), largest / len(shards))
        return jnp.repeat(jnp.exp(draws), dims[dim] // shards_of).reshape((-1,) + (1,) * (len(dims) - dim - 1))

    gain = one(*shards[0])
    for cut in shards[1:]:
        gain = gain * one(*cut)
    return gain


def centred(own_key, extent, scale, limit, shards=(), held_as=jnp.bfloat16):
    factor_of = shard_levels(own_key, extent, shards, -0.22, 0.18) if shards else 1.0
    entries = jax.random.normal(own_key, extent, jnp.float32) * scale * factor_of
    return jnp.minimum(jnp.maximum(entries, -limit), limit).astype(held_as)


def setup_inputs(seed: int = 0, part: int = 0) -> dict:
    keys = jax.random.split(jax.random.key(seed), 13)
    part_keys = jax.random.split(jax.random.fold_in(keys[12], part), 13)
    return {
        "tokens": centred(part_keys[0], (FRAMES, HEIGHT, WIDTH, D), 1.0, 6.0, ((1, 4), (2, 2))),
        "norm_gain": jnp.clip(1.0 + 0.18 * jax.random.normal(keys[1], (LAYERS, D), jnp.float32), 0.1, 1.9),
        "w_gatevals": centred(keys[2], (LAYERS, D, 2 * INNER), D ** -0.5, 0.25),
        "w_coupling": centred(keys[3], (LAYERS, D, 2 * STATE), D ** -0.5, 0.25),
        "w_steps": centred(keys[4], (LAYERS, D, HEADS), D ** -0.5, 0.25),
        "conv_values": centred(keys[5], (LAYERS, CONV, INNER), CONV ** -0.5, 3.0, (), jnp.float32),
        "conv_coupling": centred(keys[6], (LAYERS, CONV, 2 * STATE), CONV ** -0.5, 3.0, (), jnp.float32),
        "step_bias": jnp.clip(jax.random.uniform(keys[7], (LAYERS, HEADS), jnp.float32, -4.0, 0.0), -4.0, 0.0),
        "rate_log": jnp.clip(jax.random.uniform(keys[8], (LAYERS, HEADS), jnp.float32, -1.5, 1.5), -1.5, 1.5),
        "skip_gain": jnp.clip(jax.random.uniform(keys[9], (LAYERS, HEADS), jnp.float32, 0.5, 2.0), 0.5, 2.0),
        "out_gain": jnp.clip(1.0 + 0.18 * jax.random.normal(keys[10], (LAYERS, INNER), jnp.float32), 0.1, 1.9),
        "w_output": centred(keys[11], (LAYERS, INNER, D), INNER ** -0.5, 0.1875),
    }


def causal_conv(values, kernel):
    length = values.shape[1]
    taps = kernel.shape[0]
    padded = jnp.pad(values, ((0, 0), (taps - 1, 0), (0, 0)))
    total = jnp.zeros_like(values)
    for offset in range(taps):
        total = total + padded[:, offset:offset + length, :] * kernel[offset].astype(jnp.float32)
    return total

def mixer(stream, params):
    norm_gain, w_gatevals, w_coupling, w_steps, conv_values, conv_coupling, step_bias, rate_log, skip_gain, out_gain, w_output = params
    count, length, width = stream.shape
    inner = w_gatevals.shape[1] // 2
    states = w_coupling.shape[1] // 2
    heads = w_steps.shape[1]
    headdim = inner // heads
    flat = stream.reshape(count * length, width).astype(jnp.float32)
    normed = (flat * lax.rsqrt(lax.optimization_barrier(jnp.mean(flat * flat, axis=-1, keepdims=True)) + 1e-05) * norm_gain).astype(jnp.bfloat16)
    gatevals = jnp.dot(normed, w_gatevals, preferred_element_type=jnp.float32).astype(jnp.bfloat16)
    coupling = jnp.dot(normed, w_coupling, preferred_element_type=jnp.float32).astype(jnp.bfloat16)
    step_raw = jnp.dot(normed, w_steps, preferred_element_type=jnp.float32)
    gate = gatevals[:, :inner]
    values = gatevals[:, inner:]
    xs = jax.nn.silu(causal_conv(values.astype(jnp.float32).reshape(count, length, inner), conv_values)).astype(jnp.bfloat16)
    maps = jax.nn.silu(causal_conv(coupling.astype(jnp.float32).reshape(count, length, 2 * states), conv_coupling)).astype(jnp.bfloat16)
    input_map = maps[:, :, :states]
    output_map = maps[:, :, states:]
    steps = jax.nn.softplus(step_raw.reshape(count, length, heads) + step_bias)
    cumul = jnp.cumsum(steps * -jnp.exp(rate_log), axis=1).transpose(0, 2, 1)
    steps_heads = steps.transpose(0, 2, 1)
    positions = jnp.arange(length, dtype=jnp.int32)
    lower = positions[:, None] >= positions[None, :]
    spread = cumul[:, :, :, None] - cumul[:, :, None, :]
    decay = jnp.exp(jnp.where(lower[None, None, :, :], spread, -jnp.inf))
    scores = jnp.einsum('ntk,nsk->nts', output_map.astype(jnp.float32), input_map.astype(jnp.float32))
    weights = (scores[:, None, :, :] * decay * steps_heads[:, :, None, :]).astype(jnp.bfloat16)
    heads_in = xs.reshape(count, length, heads, headdim).astype(jnp.float32)
    mixed = jnp.einsum('nhts,nshp->nthp', weights.astype(jnp.float32), heads_in) + skip_gain[:, None] * heads_in
    gated = mixed.reshape(count * length, inner) * jax.nn.silu(gate.astype(jnp.float32))
    normal = (gated * lax.rsqrt(lax.optimization_barrier(jnp.mean(gated * gated, axis=-1, keepdims=True)) + 1e-05) * out_gain).astype(jnp.bfloat16)
    update = jnp.dot(normal, w_output, preferred_element_type=jnp.float32)
    return (flat + update).astype(jnp.bfloat16).reshape(count, length, width)

def sweep(stream, params):
    count, length, width = stream.shape
    block = math.gcd(count, 32)
    grouped = stream.reshape(count // block, block, length, width)
    output = lax.map(lambda piece: mixer(piece, params), grouped)
    return output.reshape(count, length, width)

def reference(tokens, norm_gain, w_gatevals, w_coupling, w_steps, conv_values, conv_coupling, step_bias, rate_log, skip_gain, out_gain, w_output):
    stacked = (norm_gain, w_gatevals, w_coupling, w_steps, conv_values, conv_coupling, step_bias, rate_log, skip_gain, out_gain, w_output)

    def params_of(index):
        return tuple((member[index] for member in stacked))
    frames, rows_all, cols_all, width = tokens.shape
    streams = tokens.transpose(1, 2, 0, 3).reshape(rows_all * cols_all, frames, width)
    current = sweep(streams, params_of(0)).reshape(rows_all, cols_all, frames, width).transpose(2, 0, 1, 3)
    streams = current.transpose(0, 2, 1, 3).reshape(frames * cols_all, rows_all, width)
    current = sweep(streams, params_of(1)).reshape(frames, cols_all, rows_all, width).transpose(0, 2, 1, 3)
    streams = current.reshape(frames * rows_all, cols_all, width)
    current = sweep(streams, params_of(2)).reshape(frames, rows_all, cols_all, width)
    return current
```

```python
import functools
import jax
import jax.numpy as jnp
from jax import lax
from jax.experimental import pallas as pl
from jax.experimental.pallas import tpu as pltpu
from jax.sharding import PartitionSpec as P


def causal_conv(values, kernel):
    length = values.shape[1]
    taps = kernel.shape[0]
    padded = jnp.pad(values, ((0, 0), (taps - 1, 0), (0, 0)))
    total = jnp.zeros_like(values)
    for offset in range(taps):
        total = total + padded[:, offset : offset + length, :] * kernel[offset]
    return total


def mixer(stream, params):
    (
        norm_gain,
        w_gatevals,
        w_coupling,
        w_steps,
        conv_values,
        conv_coupling,
        step_bias,
        rate_log,
        skip_gain,
        out_gain,
        w_output,
    ) = params
    count, length, width = stream.shape
    inner = w_gatevals.shape[1] // 2
    states = w_coupling.shape[1] // 2
    heads = w_steps.shape[1]
    headdim = inner // heads
    flat = stream.reshape(count * length, width).astype(jnp.float32)
    normed = (
        flat * lax.rsqrt(jnp.mean(flat * flat, axis=-1, keepdims=True) + 1e-05) * norm_gain
    ).astype(jnp.bfloat16)
    gatevals = jnp.dot(normed, w_gatevals, preferred_element_type=jnp.float32).astype(jnp.bfloat16)
    coupling = jnp.dot(normed, w_coupling, preferred_element_type=jnp.float32).astype(jnp.bfloat16)
    step_raw = jnp.dot(normed, w_steps, preferred_element_type=jnp.float32)
    gate = gatevals[:, :inner]
    values = gatevals[:, inner:]
    xs = jax.nn.silu(
        causal_conv(values.astype(jnp.float32).reshape(count, length, inner), conv_values)
    ).astype(jnp.bfloat16)
    maps = jax.nn.silu(
        causal_conv(coupling.astype(jnp.float32).reshape(count, length, 2 * states), conv_coupling)
    ).astype(jnp.bfloat16)
    input_map = maps[:, :, :states]
    output_map = maps[:, :, states:]
    steps = jax.nn.softplus(step_raw.reshape(count, length, heads) + step_bias)
    cumul = jnp.cumsum(steps * -jnp.exp(rate_log), axis=1).transpose(0, 2, 1)
    steps_heads = steps.transpose(0, 2, 1)
    positions = jnp.arange(length, dtype=jnp.int32)
    lower = positions[:, None] >= positions[None, :]
    spread = cumul[:, :, :, None] - cumul[:, :, None, :]
    decay = jnp.exp(jnp.where(lower[None, None, :, :], spread, -jnp.inf))
    scores = jnp.einsum("ntk,nsk->nts", output_map, input_map, preferred_element_type=jnp.float32)
    weights = (scores[:, None, :, :] * decay * steps_heads[:, :, None, :]).astype(jnp.bfloat16)
    heads_in = xs.reshape(count, length, heads, headdim)
    mixed = jnp.einsum("nhts,nshp->nthp", weights, heads_in, preferred_element_type=jnp.float32)
    mixed = mixed + skip_gain[:, None] * heads_in.astype(jnp.float32)
    gated = mixed.reshape(count * length, inner) * jax.nn.silu(gate.astype(jnp.float32))
    normal = (
        gated * lax.rsqrt(jnp.mean(gated * gated, axis=-1, keepdims=True) + 1e-05) * out_gain
    ).astype(jnp.bfloat16)
    update = jnp.dot(normal, w_output, preferred_element_type=jnp.float32)
    return (flat + update).astype(jnp.bfloat16).reshape(count, length, width)


def shards_general(
    tokens,
    norm_gain,
    w_gatevals,
    w_coupling,
    w_steps,
    conv_values,
    conv_coupling,
    step_bias,
    rate_log,
    skip_gain,
    out_gain,
    w_output,
):
    stacked = (
        norm_gain,
        w_gatevals,
        w_coupling,
        w_steps,
        conv_values,
        conv_coupling,
        step_bias,
        rate_log,
        skip_gain,
        out_gain,
        w_output,
    )

    def params_of(index):
        return tuple((member[index] for member in stacked))

    frames, rows_dev, cols_dev, width = tokens.shape
    height_devs = lax.axis_size("ha")
    width_devs = lax.axis_size("wa")
    streams = tokens.transpose(1, 2, 0, 3).reshape(rows_dev * cols_dev, frames, width)
    current = (
        mixer(streams, params_of(0))
        .reshape(rows_dev, cols_dev, frames, width)
        .transpose(2, 0, 1, 3)
    )
    piece = lax.all_to_all(current, "ha", split_axis=0, concat_axis=1, tiled=True)
    frame_part, rows_all, col_count, _ = piece.shape
    streams = piece.transpose(0, 2, 1, 3).reshape(frame_part * col_count, rows_all, width)
    output = mixer(streams, params_of(1))
    current = output.reshape(frame_part, col_count, rows_all, width).transpose(0, 2, 1, 3)
    frame_part = current.shape[0]
    rows_all = current.shape[1]
    split_rows = current.reshape(frame_part, rows_all // width_devs, width_devs, cols_dev, width)
    piece = lax.all_to_all(split_rows, "wa", split_axis=2, concat_axis=3, tiled=True)
    part_frames, row_count, single, cols_all, _ = piece.shape
    streams = piece.reshape(part_frames * row_count * single, cols_all, width)
    output = mixer(streams, params_of(2))
    current = output.reshape(part_frames, row_count, single, cols_all, width)
    row_group = rows_dev // width_devs
    arranged = current.reshape(frame_part, height_devs, row_group, width_devs, cols_dev, width)
    arranged = arranged.transpose(1, 3, 0, 2, 4, 5).reshape(
        height_devs * width_devs, frame_part, row_group, cols_dev, width
    )
    received = lax.all_to_all(arranged, ("ha", "wa"), split_axis=0, concat_axis=0, tiled=True)
    received = received.reshape(height_devs, width_devs, frame_part, row_group, cols_dev, width)
    result = received.transpose(0, 2, 3, 1, 4, 5).reshape(frames, rows_dev, cols_dev, width)
    return result


ROWS = 128
F32 = jnp.float32
BF16 = jnp.bfloat16
MESH = pl.DeviceIdType.MESH


def silu(x):
    half = 0.5 * x
    return half + half * jnp.tanh(half)


def rounded(x):
    return x.astype(BF16).astype(F32)


def project(layer, x, refs, n_block, store, wait=None):
    wg, wc, ws, ng = refs
    scale = lax.rsqrt(jnp.mean(x * x, axis=-1, keepdims=True) + 1e-05)
    normed = (x * scale * ng[layer : layer + 1, :]).astype(BF16)
    coupling = rounded(jnp.dot(normed, wc[layer], preferred_element_type=F32))
    steps = jnp.dot(normed, ws[layer], preferred_element_type=F32)
    store(None, (coupling, steps))
    total = wg.shape[2]
    for first in range(0, total, n_block):
        if wait is not None:
            wait(first // n_block)
        block = jnp.dot(normed, wg[layer, :, first : first + n_block], preferred_element_type=F32)
        store(first, rounded(block))


def mix(layer, length, stride, gate_of, value_of, coupling, steps, x, params, gated, normal):
    cv, cc, sb, rl, sk, og, wo = params
    rows = coupling.shape[0]
    heads = sb.shape[1]
    inner = cv.shape[2]
    headdim = inner // heads
    taps = cv.shape[1]
    states = coupling.shape[1] // 2
    i = lax.broadcasted_iota(jnp.int32, (rows, rows), 0)
    j = lax.broadcasted_iota(jnp.int32, (rows, rows), 1)
    if stride == 1:
        same = (i // length) == (j // length)
    else:
        same = (i % stride) == (j % stride)
    mask = same & (i >= j)

    def shift(v, by):
        if stride == 1:
            position = lax.broadcasted_iota(jnp.int32, v.shape, 0) % length
            return jnp.where(position >= by, pltpu.roll(v, by, 0), 0.0)
        pad = jnp.zeros((by * stride, v.shape[1]), v.dtype)
        return jnp.concatenate([pad, v[: rows - by * stride]], axis=0)

    def conv(v, kernel):
        total = v * kernel[taps - 1 : taps]
        for back in range(1, taps):
            total = total + shift(v, back) * kernel[taps - 1 - back : taps - back]
        return silu(total)

    maps = conv(coupling, cc[layer]).astype(BF16)
    scores = lax.dot_general(
        maps[:, states:], maps[:, :states], (((1,), (1,)), ((), ())), preferred_element_type=F32
    )
    raw = steps + sb[layer : layer + 1, :]
    steps = jnp.maximum(raw, 0.0) + jnp.log1p(jnp.exp(-jnp.abs(raw)))
    cumul = steps * -jnp.exp(rl[layer : layer + 1, :])
    by = 1
    while by < length:
        cumul = cumul + shift(cumul, by)
        by *= 2
    cumul_t = cumul.T
    steps_t = steps.T
    pair = 2 * headdim
    lane = lax.broadcasted_iota(jnp.int32, (1, pair), 1)
    squares = jnp.zeros((rows, pair), F32)
    for p in range(heads // 2):
        lanes = slice(p * pair, (p + 1) * pair)
        xs = conv(value_of(lanes), cv[layer, :, lanes]).astype(BF16).astype(F32)
        weights = []
        for h in (2 * p, 2 * p + 1):
            spread = cumul[:, h : h + 1] - cumul_t[h : h + 1, :]
            decay = jnp.exp(jnp.where(mask, spread, -jnp.inf))
            weights.append((scores * decay * steps_t[h : h + 1, :]).astype(BF16))
        both = jnp.concatenate(
            [jnp.where(lane < headdim, xs, 0.0), jnp.where(lane < headdim, 0.0, xs)], axis=0
        ).astype(BF16)
        mixed = jnp.dot(jnp.concatenate(weights, axis=1), both, preferred_element_type=F32)
        skip = jnp.where(
            lane < headdim,
            sk[layer : layer + 1, 2 * p : 2 * p + 1],
            sk[layer : layer + 1, 2 * p + 1 : 2 * p + 2],
        )
        part = (mixed + skip * xs) * silu(gate_of(lanes))
        squares = squares + part * part
        gated[:, lanes] = part
    scale = lax.rsqrt(jnp.sum(squares, axis=-1, keepdims=True) / inner + 1e-05)
    for p in range(heads // 2):
        lanes = slice(p * pair, (p + 1) * pair)
        normal[:, lanes] = (gated[:, lanes] * scale * og[layer : layer + 1, lanes]).astype(BF16)
    return x + jnp.dot(normal[...], wo[layer], preferred_element_type=F32)


def swap_matrix(outer, first, second):
    n = outer * first * second
    i = lax.broadcasted_iota(jnp.int32, (n, n), 0)
    j = lax.broadcasted_iota(jnp.int32, (n, n), 1)
    o, a, b = i // (first * second), (i // second) % first, i % second
    return jnp.where(o * first * second + b * first + a == j, 1.0, 0.0).astype(BF16)


def sweeps(
    sizes, tok_hbm, ng, wg_hbm, wc, ws, cv, cc, sb, rl, sk, og, wo_hbm, out,
    tok, wg, wo, x0, gv0, coup0, step0, gv1, x2, gv2, coup2, step2,
    landed, sent, gated, normal, back,
    tok_sem, wg_sem, wo_sem, send1, recv1, send2, recv2,
):
    ha_n, wa_n, frames, rows_dev, cols_dev, width = sizes
    peers = ha_n * wa_n
    cpc = ROWS // (frames * rows_dev)
    chunks = cols_dev // cpc
    rows_all, cols_all = rows_dev * ha_n, cols_dev * wa_n
    tokens = frames * rows_dev * cols_dev
    ha, wa = lax.axis_index("ha"), lax.axis_index("wa")
    me = ha * wa_n + wa
    blocks = wg_sem.shape[1]
    n_block = wg.shape[2] // blocks

    def device(index):
        return {"ha": index // wa_n, "wa": lax.rem(index, wa_n)}

    fetch = pltpu.make_async_copy(tok_hbm, tok, tok_sem)
    fetch.start()
    wg_copies = {}
    wo_copies = []
    layers = wg.shape[0]
    for layer in range(layers):
        for b in range(blocks):
            span = pl.ds(b * n_block, n_block)
            copy = pltpu.make_async_copy(
                wg_hbm.at[layer, :, span], wg.at[layer, :, span], wg_sem.at[layer, b]
            )
            copy.start()
            wg_copies[layer, b] = copy
        copy = pltpu.make_async_copy(wo_hbm.at[layer], wo.at[layer], wo_sem.at[layer])
        copy.start()
        wo_copies.append(copy)

    barrier = pltpu.get_barrier_semaphore()
    for k in range(1, peers):
        pl.semaphore_signal(
            barrier, inc=1, device_id=device(lax.rem(me + k, peers)), device_id_type=MESH
        )

    refs = (wg, wc, ws, ng)
    params = (cv, cc, sb, rl, sk, og, wo)
    inner = cv.shape[2]

    fetch.wait()
    swap = swap_matrix(ROWS // (rows_dev * cols_dev), cols_dev, rows_dev)
    for first in range(0, tokens, ROWS):
        part = tok[...].astype(F32).reshape(tokens, width)[first : first + ROWS].astype(BF16)
        group = ROWS // (rows_dev * cols_dev)
        x0[first // ROWS * group : (first // ROWS + 1) * group] = jnp.dot(
            swap, part, preferred_element_type=F32
        ).reshape(group, rows_dev * cols_dev, width)

    def keep_in(wide, coupling, steps):
        def store(first, value):
            if first is None:
                coupling[...] = value[0].reshape(coupling.shape)
                steps[...] = value[1].reshape(steps.shape)
            else:
                size = value.shape[1]
                wide[:, :, first : first + size] = value.reshape(wide.shape[:2] + (size,))

        return store

    project(
        0, x0[...].reshape(tokens, width), refs, n_block, keep_in(gv0, coup0, step0),
        lambda b: wg_copies[0, b].wait(),
    )
    wo_copies[0].wait()
    pl.semaphore_wait(barrier, peers - 1)

    span = rows_dev * cpc

    def view(ref, c, size):
        return lambda lanes: ref[
            :, pl.ds(pl.multiple_of(c * size, size), size), lanes
        ].reshape(ROWS, -1)

    def out1(c, k):
        peer = lax.rem(me + k, peers)
        return pltpu.make_async_remote_copy(
            src_ref=sent.at[peer, c],
            dst_ref=landed.at[c, wa, :, ha],
            send_sem=send1.at[c, k],
            recv_sem=recv1.at[c, k],
            device_id=device(peer),
            device_id_type=MESH,
        )

    def layer0(c, carry):
        pick = view(gv0, c, span)
        y = mix(
            0, frames, span,
            lambda lanes: pick(lanes),
            lambda lanes: pick(slice(inner + lanes.start, inner + lanes.stop)),
            view(coup0, c, span)(slice(None)), view(step0, c, span)(slice(None)),
            view(x0, c, span)(slice(None)),
            params, gated, normal,
        )
        sent[:, pl.ds(c, 1)] = y.reshape(frames, 1, cpc, rows_dev, width).astype(BF16)
        for k in range(1, peers):
            out1(c, k).start()
        landed[pl.ds(c, 1), pl.ds(wa, 1), :, pl.ds(ha, 1)] = sent[
            pl.ds(me, 1), pl.ds(c, 1)
        ].reshape(1, 1, cpc, 1, rows_dev, width)
        return carry

    lax.fori_loop(0, chunks, layer0, 0)

    for b in range(blocks):
        wg_copies[1, b].wait()
    wo_copies[1].wait()

    def layer1(c, carry):
        for k in range(1, peers):
            out1(c, k).wait_recv()
        x = landed[pl.ds(c, 1)].astype(F32).reshape(ROWS, width)
        held = []

        def store_part(first, value):
            if first is None:
                held.extend(value)
            else:
                gv1[:, first : first + value.shape[1]] = value

        project(1, x, refs, n_block, store_part)
        y = mix(
            1, rows_all, 1,
            lambda lanes: gv1[:, lanes],
            lambda lanes: gv1[:, inner + lanes.start : inner + lanes.stop],
            held[0], held[1], x, params, gated, normal,
        )
        y = rounded(y).reshape(wa_n, cpc, rows_all, width)
        for w in range(wa_n):
            x2[pl.ds(w * cols_dev + c * cpc, cpc)] = y[w]
        return carry

    lax.fori_loop(0, chunks, layer1, 0)

    for b in range(blocks):
        wg_copies[2, b].wait()
    wo_copies[2].wait()
    project(2, x2[...].reshape(tokens, width), refs, n_block, keep_in(gv2, coup2, step2))
    swap2 = swap_matrix(wa_n, rows_dev, cols_dev)

    def out2(j, q):
        peer_ha, peer_wa = lax.rem(ha + j + 1, ha_n), lax.rem(wa + q, wa_n)
        return pltpu.make_async_remote_copy(
            src_ref=back.at[j, peer_wa],
            dst_ref=out.at[me],
            send_sem=send2.at[j, q],
            recv_sem=recv2.at[j, q],
            device_id={"ha": peer_ha, "wa": peer_wa},
            device_id_type=MESH,
        )

    def layer2(j, carry):
        c = lax.rem(ha + j + 1, ha_n)
        pick = view(gv2, c, rows_dev)
        y = mix(
            2, cols_all, rows_dev,
            lambda lanes: pick(lanes),
            lambda lanes: pick(slice(inner + lanes.start, inner + lanes.stop)),
            view(coup2, c, rows_dev)(slice(None)), view(step2, c, rows_dev)(slice(None)),
            view(x2, c, rows_dev)(slice(None)),
            params, gated, normal,
        )
        turned = jnp.dot(swap2, y.astype(BF16), preferred_element_type=F32)
        back[pl.ds(j, 1)] = turned.reshape(1, wa_n, rows_dev, cols_dev, width).astype(BF16)
        for q in range(wa_n):
            if q == 0:
                pl.when(j < ha_n - 1)(lambda: out2(j, 0).start())
            else:
                out2(j, q).start()
        return carry

    lax.fori_loop(0, ha_n, layer2, 0)
    out[pl.ds(me, 1)] = back[ha_n - 1, pl.ds(wa, 1)]
    for j in range(ha_n):
        for q in range(wa_n):
            if j < ha_n - 1 or q > 0:
                out2(j, q).wait()
    for c in range(chunks):
        for k in range(1, peers):
            out1(c, k).wait_send()


def fits(tokens, ha_n, wa_n):
    frames, rows_dev, cols_dev, _ = tokens.shape
    return (
        frames == ha_n * wa_n
        and rows_dev == 8
        and ROWS % (frames * rows_dev) == 0
        and cols_dev % (ROWS // (frames * rows_dev)) == 0
        and (frames * rows_dev * cols_dev) % ROWS == 0
        and ROWS % (rows_dev * cols_dev) == 0
        and cols_dev * wa_n * rows_dev == ROWS
        and wa_n * (ROWS // (frames * rows_dev)) * rows_dev * ha_n == ROWS
    )


def shards(*arrays):
    tokens, ng, wg, wc, ws, cv, cc, sb, rl, sk, og, wo = arrays
    ha_n, wa_n = lax.axis_size("ha"), lax.axis_size("wa")
    if not fits(tokens, ha_n, wa_n):
        return shards_general(*arrays)
    frames, rows_dev, cols_dev, width = tokens.shape
    count = frames * rows_dev * cols_dev
    layers, _, wide = wg.shape
    inner = wide // 2
    cpc = ROWS // (frames * rows_dev)
    chunks = cols_dev // cpc
    blocks = 4
    early = (frames, rows_dev * cols_dev)
    late = (cols_dev * wa_n, rows_dev * ha_n)
    vmem = pl.BlockSpec(memory_space=pltpu.VMEM)
    hbm = pl.BlockSpec(memory_space=pl.ANY)
    sizes = (ha_n, wa_n, frames, rows_dev, cols_dev, width)
    dma = pltpu.SemaphoreType.DMA
    return pl.pallas_call(
        functools.partial(sweeps, sizes),
        out_shape=jax.ShapeDtypeStruct(tokens.shape, BF16),
        in_specs=[hbm, vmem, hbm, vmem, vmem, vmem, vmem, vmem, vmem, vmem, vmem, hbm],
        out_specs=vmem,
        scratch_shapes=[
            pltpu.VMEM(tokens.shape, BF16),
            pltpu.VMEM(wg.shape, BF16),
            pltpu.VMEM(wo.shape, BF16),
            pltpu.VMEM(early + (width,), F32),
            pltpu.VMEM(early + (wide,), F32),
            pltpu.VMEM(early + (wc.shape[2],), F32),
            pltpu.VMEM(early + (ws.shape[2],), F32),
            pltpu.VMEM((ROWS, wide), F32),
            pltpu.VMEM(late + (width,), F32),
            pltpu.VMEM(late + (wide,), F32),
            pltpu.VMEM(late + (wc.shape[2],), F32),
            pltpu.VMEM(late + (ws.shape[2],), F32),
            pltpu.VMEM((chunks, wa_n, cpc, ha_n, rows_dev, width), BF16),
            pltpu.VMEM((frames, chunks, cpc, rows_dev, width), BF16),
            pltpu.VMEM((ROWS, inner), F32),
            pltpu.VMEM((ROWS, inner), BF16),
            pltpu.VMEM((ha_n, wa_n, rows_dev, cols_dev, width), BF16),
            dma(()),
            dma((layers, blocks)),
            dma((layers,)),
            dma((chunks, ha_n * wa_n)),
            dma((chunks, ha_n * wa_n)),
            dma((ha_n, wa_n)),
            dma((ha_n, wa_n)),
        ],
        compiler_params=pltpu.CompilerParams(
            collective_id=0, has_side_effects=True, vmem_limit_bytes=48 * 2**20
        ),
    )(tokens, ng, wg, wc, ws, cv, cc, sb, rl, sk, og, wo)


def solution(mesh):
    in_specs = (P("ba", "ha", "wa", None),) + (P(),) * 11
    out_specs = P("ba", "ha", "wa", None)
    return jax.shard_map(shards, mesh=mesh, in_specs=in_specs, out_specs=out_specs, check_vma=False)
```

```python
import functools
import jax
import jax.numpy as jnp
from jax import lax
from jax.experimental import pallas as pl
from jax.experimental.pallas import tpu as pltpu
from jax.sharding import PartitionSpec as P


def causal_conv(values, kernel):
    length = values.shape[1]
    taps = kernel.shape[0]
    padded = jnp.pad(values, ((0, 0), (taps - 1, 0), (0, 0)))
    total = jnp.zeros_like(values)
    for offset in range(taps):
        total = total + padded[:, offset : offset + length, :] * kernel[offset]
    return total


def mixer(stream, params):
    (
        norm_gain,
        w_gatevals,
        w_coupling,
        w_steps,
        conv_values,
        conv_coupling,
        step_bias,
        rate_log,
        skip_gain,
        out_gain,
        w_output,
    ) = params
    count, length, width = stream.shape
    inner = w_gatevals.shape[1] // 2
    states = w_coupling.shape[1] // 2
    heads = w_steps.shape[1]
    headdim = inner // heads
    flat = stream.reshape(count * length, width).astype(jnp.float32)
    normed = (
        flat * lax.rsqrt(jnp.mean(flat * flat, axis=-1, keepdims=True) + 1e-05) * norm_gain
    ).astype(jnp.bfloat16)
    gatevals = jnp.dot(normed, w_gatevals, preferred_element_type=jnp.float32).astype(jnp.bfloat16)
    coupling = jnp.dot(normed, w_coupling, preferred_element_type=jnp.float32).astype(jnp.bfloat16)
    step_raw = jnp.dot(normed, w_steps, preferred_element_type=jnp.float32)
    gate = gatevals[:, :inner]
    values = gatevals[:, inner:]
    xs = jax.nn.silu(
        causal_conv(values.astype(jnp.float32).reshape(count, length, inner), conv_values)
    ).astype(jnp.bfloat16)
    maps = jax.nn.silu(
        causal_conv(coupling.astype(jnp.float32).reshape(count, length, 2 * states), conv_coupling)
    ).astype(jnp.bfloat16)
    input_map = maps[:, :, :states]
    output_map = maps[:, :, states:]
    steps = jax.nn.softplus(step_raw.reshape(count, length, heads) + step_bias)
    cumul = jnp.cumsum(steps * -jnp.exp(rate_log), axis=1).transpose(0, 2, 1)
    steps_heads = steps.transpose(0, 2, 1)
    positions = jnp.arange(length, dtype=jnp.int32)
    lower = positions[:, None] >= positions[None, :]
    spread = cumul[:, :, :, None] - cumul[:, :, None, :]
    decay = jnp.exp(jnp.where(lower[None, None, :, :], spread, -jnp.inf))
    scores = jnp.einsum("ntk,nsk->nts", output_map, input_map, preferred_element_type=jnp.float32)
    weights = (scores[:, None, :, :] * decay * steps_heads[:, :, None, :]).astype(jnp.bfloat16)
    heads_in = xs.reshape(count, length, heads, headdim)
    mixed = jnp.einsum("nhts,nshp->nthp", weights, heads_in, preferred_element_type=jnp.float32)
    mixed = mixed + skip_gain[:, None] * heads_in.astype(jnp.float32)
    gated = mixed.reshape(count * length, inner) * jax.nn.silu(gate.astype(jnp.float32))
    normal = (
        gated * lax.rsqrt(jnp.mean(gated * gated, axis=-1, keepdims=True) + 1e-05) * out_gain
    ).astype(jnp.bfloat16)
    update = jnp.dot(normal, w_output, preferred_element_type=jnp.float32)
    return (flat + update).astype(jnp.bfloat16).reshape(count, length, width)


def shards_general(
    tokens,
    norm_gain,
    w_gatevals,
    w_coupling,
    w_steps,
    conv_values,
    conv_coupling,
    step_bias,
    rate_log,
    skip_gain,
    out_gain,
    w_output,
):
    stacked = (
        norm_gain,
        w_gatevals,
        w_coupling,
        w_steps,
        conv_values,
        conv_coupling,
        step_bias,
        rate_log,
        skip_gain,
        out_gain,
        w_output,
    )

    def params_of(index):
        return tuple((member[index] for member in stacked))

    frames, rows_dev, cols_dev, width = tokens.shape
    height_devs = lax.axis_size("ha")
    width_devs = lax.axis_size("wa")
    streams = tokens.transpose(1, 2, 0, 3).reshape(rows_dev * cols_dev, frames, width)
    current = (
        mixer(streams, params_of(0))
        .reshape(rows_dev, cols_dev, frames, width)
        .transpose(2, 0, 1, 3)
    )
    piece = lax.all_to_all(current, "ha", split_axis=0, concat_axis=1, tiled=True)
    frame_part, rows_all, col_count, _ = piece.shape
    streams = piece.transpose(0, 2, 1, 3).reshape(frame_part * col_count, rows_all, width)
    output = mixer(streams, params_of(1))
    current = output.reshape(frame_part, col_count, rows_all, width).transpose(0, 2, 1, 3)
    frame_part = current.shape[0]
    rows_all = current.shape[1]
    split_rows = current.reshape(frame_part, rows_all // width_devs, width_devs, cols_dev, width)
    piece = lax.all_to_all(split_rows, "wa", split_axis=2, concat_axis=3, tiled=True)
    part_frames, row_count, single, cols_all, _ = piece.shape
    streams = piece.reshape(part_frames * row_count * single, cols_all, width)
    output = mixer(streams, params_of(2))
    current = output.reshape(part_frames, row_count, single, cols_all, width)
    row_group = rows_dev // width_devs
    arranged = current.reshape(frame_part, height_devs, row_group, width_devs, cols_dev, width)
    arranged = arranged.transpose(1, 3, 0, 2, 4, 5).reshape(
        height_devs * width_devs, frame_part, row_group, cols_dev, width
    )
    received = lax.all_to_all(arranged, ("ha", "wa"), split_axis=0, concat_axis=0, tiled=True)
    received = received.reshape(height_devs, width_devs, frame_part, row_group, cols_dev, width)
    result = received.transpose(0, 2, 3, 1, 4, 5).reshape(frames, rows_dev, cols_dev, width)
    return result


ROWS = 128
F32 = jnp.float32
BF16 = jnp.bfloat16
MESH = pl.DeviceIdType.MESH


def silu(x):
    half = 0.5 * x
    return half + half * jnp.tanh(half)


def rounded(x):
    return x.astype(BF16).astype(F32)


def project(layer, x, refs, n_block, store, wait=None):
    wg, wc, ws, ng = refs
    scale = lax.rsqrt(jnp.mean(x * x, axis=-1, keepdims=True) + 1e-05)
    normed = (x * scale * ng[layer : layer + 1, :]).astype(BF16)
    coupling = rounded(jnp.dot(normed, wc[layer], preferred_element_type=F32))
    steps = lax.dot_general(
        normed, ws[layer], (((1,), (1,)), ((), ())), preferred_element_type=F32
    )
    store(None, (coupling, steps))
    total = wg.shape[2]
    for first in range(0, total, n_block):
        if wait is not None:
            wait(first // n_block)
        block = jnp.dot(normed, wg[layer, :, first : first + n_block], preferred_element_type=F32)
        store(first, rounded(block))


def mix(layer, length, stride, gate_of, value_of, coupling, steps, x, params, gated, normal):
    cv, cc, sb, rl, sk, og, wo = params
    rows = coupling.shape[0]
    heads = sb.shape[1]
    inner = cv.shape[2]
    headdim = inner // heads
    taps = cv.shape[1]
    states = coupling.shape[1] // 2
    i = lax.broadcasted_iota(jnp.int32, (rows, rows), 0)
    j = lax.broadcasted_iota(jnp.int32, (rows, rows), 1)
    if stride == 1:
        same = (i // length) == (j // length)
    else:
        same = (i % stride) == (j % stride)
    mask = same & (i >= j)

    def shift(v, by):
        if stride == 1:
            position = lax.broadcasted_iota(jnp.int32, v.shape, 0) % length
            return jnp.where(position >= by, pltpu.roll(v, by, 0), 0.0)
        pad = jnp.zeros((by * stride, v.shape[1]), v.dtype)
        return jnp.concatenate([pad, v[: rows - by * stride]], axis=0)

    def conv(v, kernel):
        total = v * kernel[taps - 1 : taps]
        for back in range(1, taps):
            total = total + shift(v, back) * kernel[taps - 1 - back : taps - back]
        return silu(total)

    maps = conv(coupling, cc[layer]).astype(BF16)
    scores = lax.dot_general(
        maps[:, states:], maps[:, :states], (((1,), (1,)), ((), ())), preferred_element_type=F32
    )
    raw = steps + sb[layer : layer + 1, :]
    steps = jnp.maximum(raw, 0.0) + jnp.log1p(jnp.exp(-jnp.abs(raw)))
    cumul = steps * -jnp.exp(rl[layer : layer + 1, :])
    by = 1
    while by < length:
        cumul = cumul + shift(cumul, by)
        by *= 2
    cumul_t = cumul.T
    steps_t = steps.T
    pair = 2 * headdim
    lane = lax.broadcasted_iota(jnp.int32, (1, pair), 1)
    squares = jnp.zeros((rows, pair), F32)
    for p in range(heads // 2):
        lanes = slice(p * pair, (p + 1) * pair)
        xs = conv(value_of(lanes), cv[layer, :, lanes]).astype(BF16).astype(F32)
        weights = []
        for h in (2 * p, 2 * p + 1):
            spread = cumul[:, h : h + 1] - cumul_t[h : h + 1, :]
            decay = jnp.exp(jnp.where(mask, spread, -jnp.inf))
            weights.append((scores * decay * steps_t[h : h + 1, :]).astype(BF16))
        both = jnp.concatenate(
            [jnp.where(lane < headdim, xs, 0.0), jnp.where(lane < headdim, 0.0, xs)], axis=0
        ).astype(BF16)
        mixed = jnp.dot(jnp.concatenate(weights, axis=1), both, preferred_element_type=F32)
        skip = jnp.where(
            lane < headdim,
            sk[layer : layer + 1, 2 * p : 2 * p + 1],
            sk[layer : layer + 1, 2 * p + 1 : 2 * p + 2],
        )
        part = (mixed + skip * xs) * silu(gate_of(lanes))
        squares = squares + part * part
        gated[:, lanes] = part
    scale = lax.rsqrt(jnp.sum(squares, axis=-1, keepdims=True) / inner + 1e-05)
    for p in range(heads // 2):
        lanes = slice(p * pair, (p + 1) * pair)
        normal[:, lanes] = (gated[:, lanes] * scale * og[layer : layer + 1, lanes]).astype(BF16)
    return x + jnp.dot(normal[...], wo[layer], preferred_element_type=F32)


def swap_matrix(outer, first, second):
    n = outer * first * second
    i = lax.broadcasted_iota(jnp.int32, (n, n), 0)
    j = lax.broadcasted_iota(jnp.int32, (n, n), 1)
    o, a, b = i // (first * second), (i // second) % first, i % second
    return jnp.where(o * first * second + b * first + a == j, 1.0, 0.0).astype(BF16)


def sweeps(
    sizes, tok_hbm, ng_hbm, wg_hbm, wc_hbm, ws_hbm, cv_hbm, cc_hbm, sb_hbm, rl_hbm, sk_hbm,
    og_hbm, wo_hbm, out, tok, ng, wg, wc, ws, cv, cc, sb, rl, sk, og, wo, x0, gv0, coup0, step0, gv1, x2, gv2, coup2, step2,
    landed, sent, gated, normal, back,
    tok_sem, small_sem, wg_sem, wo_sem, send1, recv1, send2, recv2,
):
    ha_n, wa_n, frames, rows_dev, cols_dev, width = sizes
    peers = ha_n * wa_n
    cpc = ROWS // (frames * rows_dev)
    chunks = cols_dev // cpc
    rows_all, cols_all = rows_dev * ha_n, cols_dev * wa_n
    tokens = frames * rows_dev * cols_dev
    ha, wa = lax.axis_index("ha"), lax.axis_index("wa")
    me = ha * wa_n + wa
    blocks = wg_sem.shape[1]
    n_block = wg.shape[2] // blocks

    def device(index):
        return {"ha": index // wa_n, "wa": lax.rem(index, wa_n)}

    fetch = pltpu.make_async_copy(tok_hbm, tok, tok_sem)
    fetch.start()
    small = []
    for n, (src, dst) in enumerate(
        (
            (ng_hbm, ng), (wc_hbm, wc), (ws_hbm, ws), (cv_hbm, cv), (cc_hbm, cc),
            (sb_hbm, sb), (rl_hbm, rl), (sk_hbm, sk), (og_hbm, og),
        )
    ):
        copy = pltpu.make_async_copy(src, dst, small_sem.at[n])
        copy.start()
        small.append(copy)
    wg_copies = {}
    wo_copies = []
    layers = wg.shape[0]
    for layer in range(layers):
        for b in range(blocks):
            span = pl.ds(b * n_block, n_block)
            copy = pltpu.make_async_copy(
                wg_hbm.at[layer, :, span], wg.at[layer, :, span], wg_sem.at[layer, b]
            )
            copy.start()
            wg_copies[layer, b] = copy
        copy = pltpu.make_async_copy(wo_hbm.at[layer], wo.at[layer], wo_sem.at[layer])
        copy.start()
        wo_copies.append(copy)

    barrier = pltpu.get_barrier_semaphore()
    for k in range(1, peers):
        pl.semaphore_signal(
            barrier, inc=1, device_id=device(lax.rem(me + k, peers)), device_id_type=MESH
        )

    refs = (wg, wc, ws, ng)
    params = (cv, cc, sb, rl, sk, og, wo)
    inner = cv.shape[2]

    fetch.wait()
    for copy in small:
        copy.wait()
    swap = swap_matrix(ROWS // (rows_dev * cols_dev), cols_dev, rows_dev)
    for first in range(0, tokens, ROWS):
        part = tok[...].astype(F32).reshape(tokens, width)[first : first + ROWS].astype(BF16)
        group = ROWS // (rows_dev * cols_dev)
        x0[first // ROWS * group : (first // ROWS + 1) * group] = jnp.dot(
            swap, part, preferred_element_type=F32
        ).reshape(group, rows_dev * cols_dev, width)

    def keep_in(wide, coupling, steps):
        def store(first, value):
            if first is None:
                coupling[...] = value[0].reshape(coupling.shape)
                steps[...] = value[1].reshape(steps.shape)
            else:
                size = value.shape[1]
                wide[:, :, first : first + size] = value.reshape(wide.shape[:2] + (size,))

        return store

    project(
        0, x0[...].reshape(tokens, width), refs, n_block, keep_in(gv0, coup0, step0),
        lambda b: wg_copies[0, b].wait(),
    )
    wo_copies[0].wait()
    pl.semaphore_wait(barrier, peers - 1)

    span = rows_dev * cpc

    def view(ref, c, size):
        return lambda lanes: ref[
            :, pl.ds(pl.multiple_of(c * size, size), size), lanes
        ].reshape(ROWS, -1)

    def out1(c, k):
        peer = lax.rem(me + k, peers)
        return pltpu.make_async_remote_copy(
            src_ref=sent.at[peer, c],
            dst_ref=landed.at[c, wa, :, ha],
            send_sem=send1.at[c, k],
            recv_sem=recv1.at[c, k],
            device_id=device(peer),
            device_id_type=MESH,
        )

    def layer0(c, carry):
        pick = view(gv0, c, span)
        y = mix(
            0, frames, span,
            lambda lanes: pick(lanes),
            lambda lanes: pick(slice(inner + lanes.start, inner + lanes.stop)),
            view(coup0, c, span)(slice(None)), view(step0, c, span)(slice(None)),
            view(x0, c, span)(slice(None)),
            params, gated, normal,
        )
        sent[:, pl.ds(c, 1)] = y.reshape(frames, 1, cpc, rows_dev, width).astype(BF16)
        for k in range(1, peers):
            out1(c, k).start()
        landed[pl.ds(c, 1), pl.ds(wa, 1), :, pl.ds(ha, 1)] = sent[
            pl.ds(me, 1), pl.ds(c, 1)
        ].reshape(1, 1, cpc, 1, rows_dev, width)
        return carry

    lax.fori_loop(0, chunks, layer0, 0)

    for b in range(blocks):
        wg_copies[1, b].wait()
    wo_copies[1].wait()

    def layer1(c, carry):
        for k in range(1, peers):
            out1(c, k).wait_recv()
        x = landed[pl.ds(c, 1)].astype(F32).reshape(ROWS, width)
        held = []

        def store_part(first, value):
            if first is None:
                held.extend(value)
            else:
                gv1[:, first : first + value.shape[1]] = value

        project(1, x, refs, n_block, store_part)
        y = mix(
            1, rows_all, 1,
            lambda lanes: gv1[:, lanes],
            lambda lanes: gv1[:, inner + lanes.start : inner + lanes.stop],
            held[0], held[1], x, params, gated, normal,
        )
        y = rounded(y).reshape(wa_n, cpc, rows_all, width)
        for w in range(wa_n):
            x2[pl.ds(w * cols_dev + c * cpc, cpc)] = y[w]
        return carry

    lax.fori_loop(0, chunks, layer1, 0)

    for b in range(blocks):
        wg_copies[2, b].wait()
    wo_copies[2].wait()
    project(2, x2[...].reshape(tokens, width), refs, n_block, keep_in(gv2, coup2, step2))
    swap2 = swap_matrix(wa_n, rows_dev, cols_dev)

    def out2(j, q):
        peer_ha, peer_wa = lax.rem(ha + j + 1, ha_n), lax.rem(wa + q, wa_n)
        return pltpu.make_async_remote_copy(
            src_ref=back.at[j, peer_wa],
            dst_ref=out.at[me],
            send_sem=send2.at[j, q],
            recv_sem=recv2.at[j, q],
            device_id={"ha": peer_ha, "wa": peer_wa},
            device_id_type=MESH,
        )

    def layer2(j, carry):
        c = lax.rem(ha + j + 1, ha_n)
        pick = view(gv2, c, rows_dev)
        y = mix(
            2, cols_all, rows_dev,
            lambda lanes: pick(lanes),
            lambda lanes: pick(slice(inner + lanes.start, inner + lanes.stop)),
            view(coup2, c, rows_dev)(slice(None)), view(step2, c, rows_dev)(slice(None)),
            view(x2, c, rows_dev)(slice(None)),
            params, gated, normal,
        )
        turned = jnp.dot(swap2, y.astype(BF16), preferred_element_type=F32)
        back[pl.ds(j, 1)] = turned.reshape(1, wa_n, rows_dev, cols_dev, width).astype(BF16)
        for q in range(wa_n):
            if q == 0:
                pl.when(j < ha_n - 1)(lambda: out2(j, 0).start())
            else:
                out2(j, q).start()
        return carry

    lax.fori_loop(0, ha_n, layer2, 0)
    out[pl.ds(me, 1)] = back[ha_n - 1, pl.ds(wa, 1)]
    for j in range(ha_n):
        for q in range(wa_n):
            if j < ha_n - 1 or q > 0:
                out2(j, q).wait()
    for c in range(chunks):
        for k in range(1, peers):
            out1(c, k).wait_send()


def fits(tokens, ha_n, wa_n):
    frames, rows_dev, cols_dev, _ = tokens.shape
    return (
        frames == ha_n * wa_n
        and rows_dev == 8
        and ROWS % (frames * rows_dev) == 0
        and cols_dev % (ROWS // (frames * rows_dev)) == 0
        and (frames * rows_dev * cols_dev) % ROWS == 0
        and ROWS % (rows_dev * cols_dev) == 0
        and cols_dev * wa_n * rows_dev == ROWS
        and wa_n * (ROWS // (frames * rows_dev)) * rows_dev * ha_n == ROWS
    )


def shards(*arrays):
    tokens, ng, wg, wc, ws, cv, cc, sb, rl, sk, og, wo = arrays
    ha_n, wa_n = lax.axis_size("ha"), lax.axis_size("wa")
    if not fits(tokens, ha_n, wa_n):
        return shards_general(*arrays)
    ws = ws.transpose(0, 2, 1)
    frames, rows_dev, cols_dev, width = tokens.shape
    count = frames * rows_dev * cols_dev
    layers, _, wide = wg.shape
    inner = wide // 2
    cpc = ROWS // (frames * rows_dev)
    chunks = cols_dev // cpc
    blocks = 4
    early = (frames, rows_dev * cols_dev)
    late = (cols_dev * wa_n, rows_dev * ha_n)
    vmem = pl.BlockSpec(memory_space=pltpu.VMEM)
    hbm = pl.BlockSpec(memory_space=pl.ANY)
    sizes = (ha_n, wa_n, frames, rows_dev, cols_dev, width)
    dma = pltpu.SemaphoreType.DMA
    return pl.pallas_call(
        functools.partial(sweeps, sizes),
        out_shape=jax.ShapeDtypeStruct(tokens.shape, BF16),
        in_specs=[hbm] * 12,
        out_specs=vmem,
        scratch_shapes=[
            pltpu.VMEM(tokens.shape, BF16),
            *(pltpu.VMEM(a.shape, a.dtype) for a in (ng, wg, wc, ws, cv, cc, sb, rl, sk, og, wo)),
            pltpu.VMEM(early + (width,), F32),
            pltpu.VMEM(early + (wide,), F32),
            pltpu.VMEM(early + (wc.shape[2],), F32),
            pltpu.VMEM(early + (ws.shape[1],), F32),
            pltpu.VMEM((ROWS, wide), F32),
            pltpu.VMEM(late + (width,), F32),
            pltpu.VMEM(late + (wide,), F32),
            pltpu.VMEM(late + (wc.shape[2],), F32),
            pltpu.VMEM(late + (ws.shape[1],), F32),
            pltpu.VMEM((chunks, wa_n, cpc, ha_n, rows_dev, width), BF16),
            pltpu.VMEM((frames, chunks, cpc, rows_dev, width), BF16),
            pltpu.VMEM((ROWS, inner), F32),
            pltpu.VMEM((ROWS, inner), BF16),
            pltpu.VMEM((ha_n, wa_n, rows_dev, cols_dev, width), BF16),
            dma(()),
            dma((9,)),
            dma((layers, blocks)),
            dma((layers,)),
            dma((chunks, ha_n * wa_n)),
            dma((chunks, ha_n * wa_n)),
            dma((ha_n, wa_n)),
            dma((ha_n, wa_n)),
        ],
        compiler_params=pltpu.CompilerParams(
            collective_id=0, has_side_effects=True, vmem_limit_bytes=67043328
        ),
    )(tokens, ng, wg, wc, ws, cv, cc, sb, rl, sk, og, wo)


def solution(mesh):
    in_specs = (P("ba", "ha", "wa", None),) + (P(),) * 11
    out_specs = P("ba", "ha", "wa", None)
    return jax.shard_map(shards, mesh=mesh, in_specs=in_specs, out_specs=out_specs, check_vma=False)
```

```python
import functools
import jax
import jax.numpy as jnp
from jax import lax
from jax.experimental import pallas as pl
from jax.experimental.pallas import tpu as pltpu
from jax.sharding import PartitionSpec as P


def causal_conv(values, kernel):
    length = values.shape[1]
    taps = kernel.shape[0]
    padded = jnp.pad(values, ((0, 0), (taps - 1, 0), (0, 0)))
    total = jnp.zeros_like(values)
    for offset in range(taps):
        total = total + padded[:, offset : offset + length, :] * kernel[offset]
    return total


def mixer(stream, params):
    (
        norm_gain,
        w_gatevals,
        w_coupling,
        w_steps,
        conv_values,
        conv_coupling,
        step_bias,
        rate_log,
        skip_gain,
        out_gain,
        w_output,
    ) = params
    count, length, width = stream.shape
    inner = w_gatevals.shape[1] // 2
    states = w_coupling.shape[1] // 2
    heads = w_steps.shape[1]
    headdim = inner // heads
    flat = stream.reshape(count * length, width).astype(jnp.float32)
    normed = (
        flat * lax.rsqrt(jnp.mean(flat * flat, axis=-1, keepdims=True) + 1e-05) * norm_gain
    ).astype(jnp.bfloat16)
    gatevals = jnp.dot(normed, w_gatevals, preferred_element_type=jnp.float32).astype(jnp.bfloat16)
    coupling = jnp.dot(normed, w_coupling, preferred_element_type=jnp.float32).astype(jnp.bfloat16)
    step_raw = jnp.dot(normed, w_steps, preferred_element_type=jnp.float32)
    gate = gatevals[:, :inner]
    values = gatevals[:, inner:]
    xs = jax.nn.silu(
        causal_conv(values.astype(jnp.float32).reshape(count, length, inner), conv_values)
    ).astype(jnp.bfloat16)
    maps = jax.nn.silu(
        causal_conv(coupling.astype(jnp.float32).reshape(count, length, 2 * states), conv_coupling)
    ).astype(jnp.bfloat16)
    input_map = maps[:, :, :states]
    output_map = maps[:, :, states:]
    steps = jax.nn.softplus(step_raw.reshape(count, length, heads) + step_bias)
    cumul = jnp.cumsum(steps * -jnp.exp(rate_log), axis=1).transpose(0, 2, 1)
    steps_heads = steps.transpose(0, 2, 1)
    positions = jnp.arange(length, dtype=jnp.int32)
    lower = positions[:, None] >= positions[None, :]
    spread = cumul[:, :, :, None] - cumul[:, :, None, :]
    decay = jnp.exp(jnp.where(lower[None, None, :, :], spread, -jnp.inf))
    scores = jnp.einsum("ntk,nsk->nts", output_map, input_map, preferred_element_type=jnp.float32)
    weights = (scores[:, None, :, :] * decay * steps_heads[:, :, None, :]).astype(jnp.bfloat16)
    heads_in = xs.reshape(count, length, heads, headdim)
    mixed = jnp.einsum("nhts,nshp->nthp", weights, heads_in, preferred_element_type=jnp.float32)
    mixed = mixed + skip_gain[:, None] * heads_in.astype(jnp.float32)
    gated = mixed.reshape(count * length, inner) * jax.nn.silu(gate.astype(jnp.float32))
    normal = (
        gated * lax.rsqrt(jnp.mean(gated * gated, axis=-1, keepdims=True) + 1e-05) * out_gain
    ).astype(jnp.bfloat16)
    update = jnp.dot(normal, w_output, preferred_element_type=jnp.float32)
    return (flat + update).astype(jnp.bfloat16).reshape(count, length, width)


def shards_general(
    tokens,
    norm_gain,
    w_gatevals,
    w_coupling,
    w_steps,
    conv_values,
    conv_coupling,
    step_bias,
    rate_log,
    skip_gain,
    out_gain,
    w_output,
):
    stacked = (
        norm_gain,
        w_gatevals,
        w_coupling,
        w_steps,
        conv_values,
        conv_coupling,
        step_bias,
        rate_log,
        skip_gain,
        out_gain,
        w_output,
    )

    def params_of(index):
        return tuple((member[index] for member in stacked))

    frames, rows_dev, cols_dev, width = tokens.shape
    height_devs = lax.axis_size("ha")
    width_devs = lax.axis_size("wa")
    streams = tokens.transpose(1, 2, 0, 3).reshape(rows_dev * cols_dev, frames, width)
    current = (
        mixer(streams, params_of(0))
        .reshape(rows_dev, cols_dev, frames, width)
        .transpose(2, 0, 1, 3)
    )
    piece = lax.all_to_all(current, "ha", split_axis=0, concat_axis=1, tiled=True)
    frame_part, rows_all, col_count, _ = piece.shape
    streams = piece.transpose(0, 2, 1, 3).reshape(frame_part * col_count, rows_all, width)
    output = mixer(streams, params_of(1))
    current = output.reshape(frame_part, col_count, rows_all, width).transpose(0, 2, 1, 3)
    frame_part = current.shape[0]
    rows_all = current.shape[1]
    split_rows = current.reshape(frame_part, rows_all // width_devs, width_devs, cols_dev, width)
    piece = lax.all_to_all(split_rows, "wa", split_axis=2, concat_axis=3, tiled=True)
    part_frames, row_count, single, cols_all, _ = piece.shape
    streams = piece.reshape(part_frames * row_count * single, cols_all, width)
    output = mixer(streams, params_of(2))
    current = output.reshape(part_frames, row_count, single, cols_all, width)
    row_group = rows_dev // width_devs
    arranged = current.reshape(frame_part, height_devs, row_group, width_devs, cols_dev, width)
    arranged = arranged.transpose(1, 3, 0, 2, 4, 5).reshape(
        height_devs * width_devs, frame_part, row_group, cols_dev, width
    )
    received = lax.all_to_all(arranged, ("ha", "wa"), split_axis=0, concat_axis=0, tiled=True)
    received = received.reshape(height_devs, width_devs, frame_part, row_group, cols_dev, width)
    result = received.transpose(0, 2, 3, 1, 4, 5).reshape(frames, rows_dev, cols_dev, width)
    return result


ROWS = 128
F32 = jnp.float32
BF16 = jnp.bfloat16
MESH = pl.DeviceIdType.MESH


LOG2E = 1.4426950408889634


def silu_of_half(half):
    return half + half * jnp.tanh(half)


def rounded(x):
    return x.astype(BF16).astype(F32)


def project(layer, length, stride, x, refs, n_block, emit, wait=None):
    wg, wc, ws, ng, cv, cc, sb, rl = refs
    rows = x.shape[0]
    inner = cv.shape[2]
    taps = cv.shape[1]

    def shift(v, by):
        if stride == 1:
            position = lax.broadcasted_iota(jnp.int32, v.shape, 0) % length
            return jnp.where(position >= by, pltpu.roll(v, by, 0), 0.0)
        pad = jnp.zeros((by * stride, v.shape[1]), v.dtype)
        return jnp.concatenate([pad, v[: rows - by * stride]], axis=0)

    def conv(v, kernel):
        half = 0.5 * kernel
        total = v * half[taps - 1 : taps]
        for back in range(1, taps):
            total = total + shift(v, back) * half[taps - 1 - back : taps - back]
        return rounded(silu_of_half(total))

    scale = lax.rsqrt(jnp.mean(x * x, axis=-1, keepdims=True) + 1e-05)
    normed = (x * scale * ng[layer : layer + 1, :]).astype(BF16)
    coupling = rounded(jnp.dot(normed, wc[layer], preferred_element_type=F32))
    emit("maps", 0, conv(coupling, cc[layer]))
    raw = lax.dot_general(normed, ws[layer], (((1,), (1,)), ((), ())), preferred_element_type=F32)
    raw = raw + sb[layer : layer + 1, :]
    steps = jnp.maximum(raw, 0.0) + jnp.log1p(jnp.exp(-jnp.abs(raw)))
    cumul = steps * -jnp.exp(rl[layer : layer + 1, :])
    by = 1
    while by < length:
        cumul = cumul + shift(cumul, by)
        by *= 2
    cumul = cumul * LOG2E
    emit("decay", 0, cumul)
    emit("source", 0, cumul - jnp.log(steps) * LOG2E)
    for first in range(0, 2 * inner, n_block):
        if wait is not None:
            wait(first)
        block = rounded(
            jnp.dot(normed, wg[layer, :, first : first + n_block], preferred_element_type=F32)
        )
        if first < inner:
            emit("gate", first, silu_of_half(0.5 * block))
        else:
            at = first - inner
            emit("xs", at, conv(block, cv[layer, :, at : at + n_block]))


def mix(layer, length, stride, read, x, params, gated, normal):
    sk, og, wo = params
    maps, decay_to, source = read("maps"), read("decay"), read("source")
    rows, heads = decay_to.shape
    inner = og.shape[1]
    headdim = inner // heads
    states = maps.shape[1] // 2
    i = lax.broadcasted_iota(jnp.int32, (rows, rows), 0)
    j = lax.broadcasted_iota(jnp.int32, (rows, rows), 1)
    if stride == 1:
        same = (i // length) == (j // length)
    else:
        same = (i % stride) == (j % stride)
    mask = same & (i >= j)
    maps = maps.astype(BF16)
    scores = lax.dot_general(
        maps[:, states:], maps[:, :states], (((1,), (1,)), ((), ())), preferred_element_type=F32
    )
    source_t = source.T
    pair = 2 * headdim
    lane = lax.broadcasted_iota(jnp.int32, (1, pair), 1)
    squares = jnp.zeros((rows, pair), F32)
    for p in range(heads // 2):
        lanes = slice(p * pair, (p + 1) * pair)
        xs = read("xs", lanes)
        weights = []
        for h in (2 * p, 2 * p + 1):
            spread = decay_to[:, h : h + 1] - source_t[h : h + 1, :]
            decay = jnp.exp2(jnp.where(mask, spread, -jnp.inf))
            weights.append((scores * decay).astype(BF16))
        both = jnp.concatenate(
            [jnp.where(lane < headdim, xs, 0.0), jnp.where(lane < headdim, 0.0, xs)], axis=0
        ).astype(BF16)
        mixed = jnp.dot(jnp.concatenate(weights, axis=1), both, preferred_element_type=F32)
        skip = jnp.where(
            lane < headdim,
            sk[layer : layer + 1, 2 * p : 2 * p + 1],
            sk[layer : layer + 1, 2 * p + 1 : 2 * p + 2],
        )
        part = (mixed + skip * xs) * read("gate", lanes)
        squares = squares + part * part
        gated[:, lanes] = part
    scale = lax.rsqrt(jnp.sum(squares, axis=-1, keepdims=True) / inner + 1e-05)
    for p in range(heads // 2):
        lanes = slice(p * pair, (p + 1) * pair)
        normal[:, lanes] = (gated[:, lanes] * scale * og[layer : layer + 1, lanes]).astype(BF16)
    return x + jnp.dot(normal[...], wo[layer], preferred_element_type=F32)


def swap_matrix(outer, first, second):
    n = outer * first * second
    i = lax.broadcasted_iota(jnp.int32, (n, n), 0)
    j = lax.broadcasted_iota(jnp.int32, (n, n), 1)
    o, a, b = i // (first * second), (i // second) % first, i % second
    return jnp.where(o * first * second + b * first + a == j, 1.0, 0.0).astype(BF16)


def sweeps(
    sizes, tok_hbm, ng_hbm, wg_hbm, wc_hbm, ws_hbm, cv_hbm, cc_hbm, sb_hbm, rl_hbm, sk_hbm,
    og_hbm, wo_hbm, out, tok, ng, wg, wc, ws, cv, cc, sb, rl, sk, og, wo, x0, x2,
    gate0, xs0, maps0, decay0, source0, gate1, xs1, maps1, decay1, source1,
    gate2, xs2, maps2, decay2, source2,
    landed, sent, gated, normal, back,
    tok_sem, small_sem, wg_sem, wo_sem, send1, recv1, send2, recv2,
):
    ha_n, wa_n, frames, rows_dev, cols_dev, width, group1 = sizes
    peers = ha_n * wa_n
    cpc = ROWS // (frames * rows_dev)
    chunks = cols_dev // cpc
    rows_all, cols_all = rows_dev * ha_n, cols_dev * wa_n
    tokens = frames * rows_dev * cols_dev
    ha, wa = lax.axis_index("ha"), lax.axis_index("wa")
    me = ha * wa_n + wa
    blocks = wg_sem.shape[1]
    n_block = wg.shape[2] // blocks
    n_dot = n_block // 2

    def device(index):
        return {"ha": index // wa_n, "wa": lax.rem(index, wa_n)}

    fetch = pltpu.make_async_copy(tok_hbm, tok, tok_sem)
    fetch.start()
    small = []
    for n, (src, dst) in enumerate(
        (
            (ng_hbm, ng), (wc_hbm, wc), (ws_hbm, ws), (cv_hbm, cv), (cc_hbm, cc),
            (sb_hbm, sb), (rl_hbm, rl), (sk_hbm, sk), (og_hbm, og),
        )
    ):
        copy = pltpu.make_async_copy(src, dst, small_sem.at[n])
        copy.start()
        small.append(copy)
    wg_copies = {}
    wo_copies = []
    layers = wg.shape[0]
    for layer in range(layers):
        for b in range(blocks):
            span = pl.ds(b * n_block, n_block)
            copy = pltpu.make_async_copy(
                wg_hbm.at[layer, :, span], wg.at[layer, :, span], wg_sem.at[layer, b]
            )
            copy.start()
            wg_copies[layer, b] = copy
        copy = pltpu.make_async_copy(wo_hbm.at[layer], wo.at[layer], wo_sem.at[layer])
        copy.start()
        wo_copies.append(copy)

    barrier = pltpu.get_barrier_semaphore()
    for k in range(1, peers):
        pl.semaphore_signal(
            barrier, inc=1, device_id=device(lax.rem(me + k, peers)), device_id_type=MESH
        )

    refs = (wg, wc, ws, ng, cv, cc, sb, rl)
    params = (sk, og, wo)
    names = ("gate", "xs", "maps", "decay", "source")
    kept0 = dict(zip(names, (gate0, xs0, maps0, decay0, source0)))
    kept1 = dict(zip(names, (gate1, xs1, maps1, decay1, source1)))
    kept2 = dict(zip(names, (gate2, xs2, maps2, decay2, source2)))

    fetch.wait()
    for copy in small:
        copy.wait()
    swap = swap_matrix(ROWS // (rows_dev * cols_dev), cols_dev, rows_dev)
    for first in range(0, tokens, ROWS):
        part = tok[...].astype(F32).reshape(tokens, width)[first : first + ROWS].astype(BF16)
        group = ROWS // (rows_dev * cols_dev)
        x0[first // ROWS * group : (first // ROWS + 1) * group] = jnp.dot(
            swap, part, preferred_element_type=F32
        ).reshape(group, rows_dev * cols_dev, width)

    def keep_in(kept):
        def emit(name, first, value):
            ref = kept[name]
            size = value.shape[1]
            ref[:, :, first : first + size] = value.reshape(ref.shape[:2] + (size,))

        return emit

    def wait0(first):
        if first % n_block == 0:
            wg_copies[0, first // n_block].wait()

    project(
        0, frames, rows_dev * cols_dev, x0[...].reshape(tokens, width), refs, n_dot,
        keep_in(kept0), wait0,
    )
    wo_copies[0].wait()
    pl.semaphore_wait(barrier, peers - 1)

    span = rows_dev * cpc

    def view(kept, c, size):
        part = pl.ds(pl.multiple_of(c * size, size), size)
        return lambda name, lanes=slice(None): kept[name][:, part, lanes].reshape(ROWS, -1)

    def out1(c, k):
        peer = lax.rem(me + k, peers)
        return pltpu.make_async_remote_copy(
            src_ref=sent.at[peer, c],
            dst_ref=landed.at[c, wa, :, ha],
            send_sem=send1.at[c, k],
            recv_sem=recv1.at[c, k],
            device_id=device(peer),
            device_id_type=MESH,
        )

    def layer0(c, carry):
        y = mix(
            0, frames, span, view(kept0, c, span), view({"x": x0}, c, span)("x"),
            params, gated, normal,
        )
        sent[:, pl.ds(c, 1)] = y.reshape(frames, 1, cpc, rows_dev, width).astype(BF16)
        for k in range(1, peers):
            out1(c, k).start()
        landed[pl.ds(c, 1), pl.ds(wa, 1), :, pl.ds(ha, 1)] = sent[
            pl.ds(me, 1), pl.ds(c, 1)
        ].reshape(1, 1, cpc, 1, rows_dev, width)
        return carry

    lax.fori_loop(0, chunks, layer0, 0)

    for b in range(blocks):
        wg_copies[1, b].wait()
    wo_copies[1].wait()

    def layer1(half, carry):
        for part in range(group1):
            for k in range(1, peers):
                out1(half * group1 + part, k).wait_recv()
        x = landed[pl.ds(half * group1, group1)].astype(F32).reshape(group1 * ROWS, width)

        def emit(name, first, value):
            kept1[name][:, first : first + value.shape[1]] = value

        project(1, rows_all, 1, x, refs, n_dot, emit)
        for part in range(group1):
            layer1_mix(half * group1 + part, part * ROWS)
        return carry

    def layer1_mix(c, first):
        x = landed[pl.ds(c, 1)].astype(F32).reshape(ROWS, width)
        y = mix(
            1, rows_all, 1,
            lambda name, lanes=slice(None): kept1[name][first : first + ROWS, lanes],
            x, params, gated, normal,
        )
        y = rounded(y).reshape(wa_n, cpc, rows_all, width)
        for w in range(wa_n):
            x2[pl.ds(w * cols_dev + c * cpc, cpc)] = y[w]

    lax.fori_loop(0, chunks // group1, layer1, 0)

    for b in range(blocks):
        wg_copies[2, b].wait()
    wo_copies[2].wait()
    project(
        2, cols_all, rows_all, x2[...].reshape(tokens, width), refs, n_dot, keep_in(kept2)
    )
    swap2 = swap_matrix(wa_n, rows_dev, cols_dev)

    def out2(j, q):
        peer_ha, peer_wa = lax.rem(ha + j + 1, ha_n), lax.rem(wa + q, wa_n)
        return pltpu.make_async_remote_copy(
            src_ref=back.at[j, peer_wa],
            dst_ref=out.at[me],
            send_sem=send2.at[j, q],
            recv_sem=recv2.at[j, q],
            device_id={"ha": peer_ha, "wa": peer_wa},
            device_id_type=MESH,
        )

    def layer2(j, carry):
        c = lax.rem(ha + j + 1, ha_n)
        y = mix(
            2, cols_all, rows_dev, view(kept2, c, rows_dev), view({"x": x2}, c, rows_dev)("x"),
            params, gated, normal,
        )
        turned = jnp.dot(swap2, y.astype(BF16), preferred_element_type=F32)
        back[pl.ds(j, 1)] = turned.reshape(1, wa_n, rows_dev, cols_dev, width).astype(BF16)
        for q in range(wa_n):
            if q == 0:
                pl.when(j < ha_n - 1)(lambda: out2(j, 0).start())
            else:
                out2(j, q).start()
        return carry

    lax.fori_loop(0, ha_n, layer2, 0)
    out[pl.ds(me, 1)] = back[ha_n - 1, pl.ds(wa, 1)]
    for j in range(ha_n):
        for q in range(wa_n):
            if j < ha_n - 1 or q > 0:
                out2(j, q).wait()
    for c in range(chunks):
        for k in range(1, peers):
            out1(c, k).wait_send()


def fits(tokens, ha_n, wa_n):
    frames, rows_dev, cols_dev, _ = tokens.shape
    return (
        frames == ha_n * wa_n
        and rows_dev == 8
        and ROWS % (frames * rows_dev) == 0
        and cols_dev % (ROWS // (frames * rows_dev)) == 0
        and (frames * rows_dev * cols_dev) % ROWS == 0
        and ROWS % (rows_dev * cols_dev) == 0
        and cols_dev * wa_n * rows_dev == ROWS
        and wa_n * (ROWS // (frames * rows_dev)) * rows_dev * ha_n == ROWS
    )


def shards(*arrays):
    tokens, ng, wg, wc, ws, cv, cc, sb, rl, sk, og, wo = arrays
    ha_n, wa_n = lax.axis_size("ha"), lax.axis_size("wa")
    if not fits(tokens, ha_n, wa_n):
        return shards_general(*arrays)
    ws = ws.transpose(0, 2, 1)
    frames, rows_dev, cols_dev, width = tokens.shape
    count = frames * rows_dev * cols_dev
    layers, _, wide = wg.shape
    inner = wide // 2
    cpc = ROWS // (frames * rows_dev)
    chunks = cols_dev // cpc
    blocks = 4
    group1 = 2 if chunks % 2 == 0 else 1
    early = (frames, rows_dev * cols_dev)
    late = (cols_dev * wa_n, rows_dev * ha_n)
    vmem = pl.BlockSpec(memory_space=pltpu.VMEM)
    hbm = pl.BlockSpec(memory_space=pl.ANY)
    sizes = (ha_n, wa_n, frames, rows_dev, cols_dev, width, group1)
    dma = pltpu.SemaphoreType.DMA
    return pl.pallas_call(
        functools.partial(sweeps, sizes),
        out_shape=jax.ShapeDtypeStruct(tokens.shape, BF16),
        in_specs=[hbm] * 12,
        out_specs=vmem,
        scratch_shapes=[
            pltpu.VMEM(tokens.shape, BF16),
            *(pltpu.VMEM(a.shape, a.dtype) for a in (ng, wg, wc, ws, cv, cc, sb, rl, sk, og, wo)),
            pltpu.VMEM(early + (width,), F32),
            pltpu.VMEM(late + (width,), F32),
            *(
                pltpu.VMEM(lead + (size,), F32)
                for lead in (early, (group1 * ROWS,), late)
                for size in (inner, inner, wc.shape[2], ws.shape[1], ws.shape[1])
            ),
            pltpu.VMEM((chunks, wa_n, cpc, ha_n, rows_dev, width), BF16),
            pltpu.VMEM((frames, chunks, cpc, rows_dev, width), BF16),
            pltpu.VMEM((ROWS, inner), F32),
            pltpu.VMEM((ROWS, inner), BF16),
            pltpu.VMEM((ha_n, wa_n, rows_dev, cols_dev, width), BF16),
            dma(()),
            dma((9,)),
            dma((layers, blocks)),
            dma((layers,)),
            dma((chunks, ha_n * wa_n)),
            dma((chunks, ha_n * wa_n)),
            dma((ha_n, wa_n)),
            dma((ha_n, wa_n)),
        ],
        compiler_params=pltpu.CompilerParams(
            collective_id=0, has_side_effects=True, vmem_limit_bytes=67043328
        ),
    )(tokens, ng, wg, wc, ws, cv, cc, sb, rl, sk, og, wo)


def solution(mesh):
    in_specs = (P("ba", "ha", "wa", None),) + (P(),) * 11
    out_specs = P("ba", "ha", "wa", None)
    return jax.shard_map(shards, mesh=mesh, in_specs=in_specs, out_specs=out_specs, check_vma=False)
```

```python
import functools
import jax
import jax.numpy as jnp
from jax import lax
from jax.experimental import pallas as pl
from jax.experimental.pallas import tpu as pltpu
from jax.sharding import PartitionSpec as P


def causal_conv(values, kernel):
    length = values.shape[1]
    taps = kernel.shape[0]
    padded = jnp.pad(values, ((0, 0), (taps - 1, 0), (0, 0)))
    total = jnp.zeros_like(values)
    for offset in range(taps):
        total = total + padded[:, offset : offset + length, :] * kernel[offset]
    return total


def mixer(stream, params):
    (
        norm_gain,
        w_gatevals,
        w_coupling,
        w_steps,
        conv_values,
        conv_coupling,
        step_bias,
        rate_log,
        skip_gain,
        out_gain,
        w_output,
    ) = params
    count, length, width = stream.shape
    inner = w_gatevals.shape[1] // 2
    states = w_coupling.shape[1] // 2
    heads = w_steps.shape[1]
    headdim = inner // heads
    flat = stream.reshape(count * length, width).astype(jnp.float32)
    normed = (
        flat * lax.rsqrt(jnp.mean(flat * flat, axis=-1, keepdims=True) + 1e-05) * norm_gain
    ).astype(jnp.bfloat16)
    gatevals = jnp.dot(normed, w_gatevals, preferred_element_type=jnp.float32).astype(jnp.bfloat16)
    coupling = jnp.dot(normed, w_coupling, preferred_element_type=jnp.float32).astype(jnp.bfloat16)
    step_raw = jnp.dot(normed, w_steps, preferred_element_type=jnp.float32)
    gate = gatevals[:, :inner]
    values = gatevals[:, inner:]
    xs = jax.nn.silu(
        causal_conv(values.astype(jnp.float32).reshape(count, length, inner), conv_values)
    ).astype(jnp.bfloat16)
    maps = jax.nn.silu(
        causal_conv(coupling.astype(jnp.float32).reshape(count, length, 2 * states), conv_coupling)
    ).astype(jnp.bfloat16)
    input_map = maps[:, :, :states]
    output_map = maps[:, :, states:]
    steps = jax.nn.softplus(step_raw.reshape(count, length, heads) + step_bias)
    cumul = jnp.cumsum(steps * -jnp.exp(rate_log), axis=1).transpose(0, 2, 1)
    steps_heads = steps.transpose(0, 2, 1)
    positions = jnp.arange(length, dtype=jnp.int32)
    lower = positions[:, None] >= positions[None, :]
    spread = cumul[:, :, :, None] - cumul[:, :, None, :]
    decay = jnp.exp(jnp.where(lower[None, None, :, :], spread, -jnp.inf))
    scores = jnp.einsum("ntk,nsk->nts", output_map, input_map, preferred_element_type=jnp.float32)
    weights = (scores[:, None, :, :] * decay * steps_heads[:, :, None, :]).astype(jnp.bfloat16)
    heads_in = xs.reshape(count, length, heads, headdim)
    mixed = jnp.einsum("nhts,nshp->nthp", weights, heads_in, preferred_element_type=jnp.float32)
    mixed = mixed + skip_gain[:, None] * heads_in.astype(jnp.float32)
    gated = mixed.reshape(count * length, inner) * jax.nn.silu(gate.astype(jnp.float32))
    normal = (
        gated * lax.rsqrt(jnp.mean(gated * gated, axis=-1, keepdims=True) + 1e-05) * out_gain
    ).astype(jnp.bfloat16)
    update = jnp.dot(normal, w_output, preferred_element_type=jnp.float32)
    return (flat + update).astype(jnp.bfloat16).reshape(count, length, width)


def shards_general(
    tokens,
    norm_gain,
    w_gatevals,
    w_coupling,
    w_steps,
    conv_values,
    conv_coupling,
    step_bias,
    rate_log,
    skip_gain,
    out_gain,
    w_output,
):
    stacked = (
        norm_gain,
        w_gatevals,
        w_coupling,
        w_steps,
        conv_values,
        conv_coupling,
        step_bias,
        rate_log,
        skip_gain,
        out_gain,
        w_output,
    )

    def params_of(index):
        return tuple((member[index] for member in stacked))

    frames, rows_dev, cols_dev, width = tokens.shape
    height_devs = lax.axis_size("ha")
    width_devs = lax.axis_size("wa")
    streams = tokens.transpose(1, 2, 0, 3).reshape(rows_dev * cols_dev, frames, width)
    current = (
        mixer(streams, params_of(0))
        .reshape(rows_dev, cols_dev, frames, width)
        .transpose(2, 0, 1, 3)
    )
    piece = lax.all_to_all(current, "ha", split_axis=0, concat_axis=1, tiled=True)
    frame_part, rows_all, col_count, _ = piece.shape
    streams = piece.transpose(0, 2, 1, 3).reshape(frame_part * col_count, rows_all, width)
    output = mixer(streams, params_of(1))
    current = output.reshape(frame_part, col_count, rows_all, width).transpose(0, 2, 1, 3)
    frame_part = current.shape[0]
    rows_all = current.shape[1]
    split_rows = current.reshape(frame_part, rows_all // width_devs, width_devs, cols_dev, width)
    piece = lax.all_to_all(split_rows, "wa", split_axis=2, concat_axis=3, tiled=True)
    part_frames, row_count, single, cols_all, _ = piece.shape
    streams = piece.reshape(part_frames * row_count * single, cols_all, width)
    output = mixer(streams, params_of(2))
    current = output.reshape(part_frames, row_count, single, cols_all, width)
    row_group = rows_dev // width_devs
    arranged = current.reshape(frame_part, height_devs, row_group, width_devs, cols_dev, width)
    arranged = arranged.transpose(1, 3, 0, 2, 4, 5).reshape(
        height_devs * width_devs, frame_part, row_group, cols_dev, width
    )
    received = lax.all_to_all(arranged, ("ha", "wa"), split_axis=0, concat_axis=0, tiled=True)
    received = received.reshape(height_devs, width_devs, frame_part, row_group, cols_dev, width)
    result = received.transpose(0, 2, 3, 1, 4, 5).reshape(frames, rows_dev, cols_dev, width)
    return result


ROWS = 128
F32 = jnp.float32
BF16 = jnp.bfloat16
MESH = pl.DeviceIdType.MESH


LOG2E = 1.4426950408889634


def silu_of_half(half):
    return half + half * jnp.tanh(half)


def rounded(x):
    return x.astype(BF16).astype(F32)


def project(layer, length, stride, x, refs, n_block, emit, wait=None):
    wg, wc, ws, ng, cv, cc, sb, rl = refs
    rows = x.shape[0]
    inner = cv.shape[2]
    taps = cv.shape[1]

    def shift(v, by):
        if stride == 1:
            position = lax.broadcasted_iota(jnp.int32, v.shape, 0) % length
            return jnp.where(position >= by, pltpu.roll(v, by, 0), 0.0)
        pad = jnp.zeros((by * stride, v.shape[1]), v.dtype)
        return jnp.concatenate([pad, v[: rows - by * stride]], axis=0)

    def conv(v, kernel):
        half = 0.5 * kernel
        total = v * half[taps - 1 : taps]
        for back in range(1, taps):
            total = total + shift(v, back) * half[taps - 1 - back : taps - back]
        return rounded(silu_of_half(total))

    scale = lax.rsqrt(jnp.mean(x * x, axis=-1, keepdims=True) + 1e-05)
    normed = (x * scale * ng[layer : layer + 1, :]).astype(BF16)
    coupling = rounded(jnp.dot(normed, wc[layer], preferred_element_type=F32))
    emit("maps", 0, conv(coupling, cc[layer]))
    raw = lax.dot_general(normed, ws[layer], (((1,), (1,)), ((), ())), preferred_element_type=F32)
    raw = raw + sb[layer : layer + 1, :]
    steps = jnp.maximum(raw, 0.0) + jnp.log1p(jnp.exp(-jnp.abs(raw)))
    cumul = steps * -jnp.exp(rl[layer : layer + 1, :])
    by = 1
    while by < length:
        cumul = cumul + shift(cumul, by)
        by *= 2
    cumul = cumul * LOG2E
    emit("decay", 0, cumul)
    emit("source", 0, cumul - jnp.log(steps) * LOG2E)
    for first in range(0, 2 * inner, n_block):
        if wait is not None:
            wait(first)
        block = rounded(
            jnp.dot(normed, wg[layer, :, first : first + n_block], preferred_element_type=F32)
        )
        if first < inner:
            emit("gate", first, silu_of_half(0.5 * block))
        else:
            at = first - inner
            emit("xs", at, conv(block, cv[layer, :, at : at + n_block]))


def mix(layer, length, stride, read, x, params, gated, normal):
    sk, og, wo = params
    maps, decay_to, source = read("maps"), read("decay"), read("source")
    rows, heads = decay_to.shape
    inner = og.shape[1]
    headdim = inner // heads
    states = maps.shape[1] // 2
    i = lax.broadcasted_iota(jnp.int32, (rows, rows), 0)
    j = lax.broadcasted_iota(jnp.int32, (rows, rows), 1)
    if stride == 1:
        same = (i // length) == (j // length)
    else:
        same = (i % stride) == (j % stride)
    mask = same & (i >= j)
    maps = maps.astype(BF16)
    scores = lax.dot_general(
        maps[:, states:], maps[:, :states], (((1,), (1,)), ((), ())), preferred_element_type=F32
    )
    source_t = source.T
    pair = 2 * headdim
    lane = lax.broadcasted_iota(jnp.int32, (1, pair), 1)
    squares = jnp.zeros((rows, pair), F32)
    for p in range(heads // 2):
        lanes = slice(p * pair, (p + 1) * pair)
        xs = read("xs", lanes)
        weights = []
        for h in (2 * p, 2 * p + 1):
            spread = decay_to[:, h : h + 1] - source_t[h : h + 1, :]
            decay = jnp.exp2(jnp.where(mask, spread, -jnp.inf))
            weights.append((scores * decay).astype(BF16))
        both = jnp.concatenate(
            [jnp.where(lane < headdim, xs, 0.0), jnp.where(lane < headdim, 0.0, xs)], axis=0
        ).astype(BF16)
        mixed = jnp.dot(jnp.concatenate(weights, axis=1), both, preferred_element_type=F32)
        skip = jnp.where(
            lane < headdim,
            sk[layer : layer + 1, 2 * p : 2 * p + 1],
            sk[layer : layer + 1, 2 * p + 1 : 2 * p + 2],
        )
        part = (mixed + skip * xs) * read("gate", lanes)
        squares = squares + part * part
        gated[:, lanes] = part
    scale = lax.rsqrt(jnp.sum(squares, axis=-1, keepdims=True) / inner + 1e-05)
    for p in range(heads // 2):
        lanes = slice(p * pair, (p + 1) * pair)
        normal[:, lanes] = (gated[:, lanes] * scale * og[layer : layer + 1, lanes]).astype(BF16)
    return x + jnp.dot(normal[...], wo[layer], preferred_element_type=F32)


def swap_matrix(outer, first, second):
    n = outer * first * second
    i = lax.broadcasted_iota(jnp.int32, (n, n), 0)
    j = lax.broadcasted_iota(jnp.int32, (n, n), 1)
    o, a, b = i // (first * second), (i // second) % first, i % second
    return jnp.where(o * first * second + b * first + a == j, 1.0, 0.0).astype(BF16)


def sweeps(
    sizes, tok_hbm, ng_hbm, wg_hbm, wc_hbm, ws_hbm, cv_hbm, cc_hbm, sb_hbm, rl_hbm, sk_hbm,
    og_hbm, wo_hbm, out, tok, ng, wg, wc, ws, cv, cc, sb, rl, sk, og, wo, x0, x2,
    gate, xs, maps, decay, source,
    landed, sent, gated, normal, back,
    tok_sem, small_sem, wg_sem, wo_sem, send1, recv1, send2, recv2,
):
    ha_n, wa_n, frames, rows_dev, cols_dev, width = sizes
    peers = ha_n * wa_n
    cpc = ROWS // (frames * rows_dev)
    chunks = cols_dev // cpc
    rows_all, cols_all = rows_dev * ha_n, cols_dev * wa_n
    tokens = frames * rows_dev * cols_dev
    ha, wa = lax.axis_index("ha"), lax.axis_index("wa")
    me = ha * wa_n + wa
    blocks = wg_sem.shape[1]
    n_block = wg.shape[2] // blocks
    n_dot = n_block // 2

    def device(index):
        return {"ha": index // wa_n, "wa": lax.rem(index, wa_n)}

    fetch = pltpu.make_async_copy(tok_hbm, tok, tok_sem)
    fetch.start()
    small = []
    for n, (src, dst) in enumerate(
        (
            (ng_hbm, ng), (wc_hbm, wc), (ws_hbm, ws), (cv_hbm, cv), (cc_hbm, cc),
            (sb_hbm, sb), (rl_hbm, rl), (sk_hbm, sk), (og_hbm, og),
        )
    ):
        copy = pltpu.make_async_copy(src, dst, small_sem.at[n])
        copy.start()
        small.append(copy)
    wg_copies = {}
    wo_copies = []
    layers = wg.shape[0]

    def start_weights(layer):
        for b in range(blocks):
            span = pl.ds(b * n_block, n_block)
            copy = pltpu.make_async_copy(
                wg_hbm.at[layer, :, span], wg.at[layer, :, span], wg_sem.at[layer, b]
            )
            copy.start()
            wg_copies[layer, b] = copy
        copy = pltpu.make_async_copy(wo_hbm.at[layer], wo.at[layer], wo_sem.at[layer])
        copy.start()
        wo_copies.append(copy)

    start_weights(0)

    barrier = pltpu.get_barrier_semaphore()
    for k in range(1, peers):
        pl.semaphore_signal(
            barrier, inc=1, device_id=device(lax.rem(me + k, peers)), device_id_type=MESH
        )

    refs = (wg, wc, ws, ng, cv, cc, sb, rl)
    params = (sk, og, wo)
    kept = dict(gate=gate, xs=xs, maps=maps, decay=decay, source=source)

    def emit(name, first, value):
        kept[name][:, first : first + value.shape[1]] = value

    def read(name, lanes=slice(None)):
        return kept[name][:, lanes]

    def run(layer, length, stride, x):
        project(layer, length, stride, x, refs, n_dot, emit)
        return mix(layer, length, stride, read, x, params, gated, normal)

    fetch.wait()
    for copy in small:
        copy.wait()
    swap = swap_matrix(ROWS // (rows_dev * cols_dev), cols_dev, rows_dev)
    for first in range(0, tokens, ROWS):
        part = tok[...].astype(F32).reshape(tokens, width)[first : first + ROWS].astype(BF16)
        group = ROWS // (rows_dev * cols_dev)
        x0[first // ROWS * group : (first // ROWS + 1) * group] = jnp.dot(
            swap, part, preferred_element_type=F32
        ).reshape(group, rows_dev * cols_dev, width)

    for b in range(blocks):
        wg_copies[0, b].wait()
    wo_copies[0].wait()
    for layer in range(1, layers):
        start_weights(layer)
    pl.semaphore_wait(barrier, peers - 1)

    span = rows_dev * cpc

    def view(ref, c, size):
        return ref[:, pl.ds(pl.multiple_of(c * size, size), size), :].reshape(ROWS, width)

    def out1(c, k):
        peer = lax.rem(me + k, peers)
        return pltpu.make_async_remote_copy(
            src_ref=sent.at[peer, c],
            dst_ref=landed.at[c, wa, :, ha],
            send_sem=send1.at[c, k],
            recv_sem=recv1.at[c, k],
            device_id=device(peer),
            device_id_type=MESH,
        )

    def layer0(c, carry):
        y = run(0, frames, span, view(x0, c, span))
        sent[:, pl.ds(c, 1)] = y.reshape(frames, 1, cpc, rows_dev, width).astype(BF16)
        for k in range(1, peers):
            out1(c, k).start()
        landed[pl.ds(c, 1), pl.ds(wa, 1), :, pl.ds(ha, 1)] = sent[
            pl.ds(me, 1), pl.ds(c, 1)
        ].reshape(1, 1, cpc, 1, rows_dev, width)
        return carry

    lax.fori_loop(0, chunks, layer0, 0)

    for b in range(blocks):
        wg_copies[1, b].wait()
    wo_copies[1].wait()

    def layer1(c, carry):
        for k in range(1, peers):
            out1(c, k).wait_recv()
        y = run(1, rows_all, 1, landed[pl.ds(c, 1)].astype(F32).reshape(ROWS, width))
        y = rounded(y).reshape(wa_n, cpc, rows_all, width)
        for w in range(wa_n):
            x2[pl.ds(w * cols_dev + c * cpc, cpc)] = y[w]
        return carry

    lax.fori_loop(0, chunks, layer1, 0)

    for b in range(blocks):
        wg_copies[2, b].wait()
    wo_copies[2].wait()
    swap2 = swap_matrix(wa_n, rows_dev, cols_dev)

    def target(j):
        if ha_n != 4:
            return lax.rem(ha + j + 1, ha_n)
        mirrored = ha + ((j + 1) // 2 % 2) * (ha_n - 1 - 2 * ha)
        return lax.rem(mirrored + (1 - j % 2) * (ha_n // 2), ha_n)

    def out2(j, q):
        peer_ha, peer_wa = target(j), lax.rem(wa + q, wa_n)
        return pltpu.make_async_remote_copy(
            src_ref=back.at[j, peer_wa],
            dst_ref=out.at[me],
            send_sem=send2.at[j, q],
            recv_sem=recv2.at[j, q],
            device_id={"ha": peer_ha, "wa": peer_wa},
            device_id_type=MESH,
        )

    def layer2(j, carry):
        c = target(j)
        y = run(2, cols_all, rows_dev, view(x2, c, rows_dev))
        turned = jnp.dot(swap2, y.astype(BF16), preferred_element_type=F32)
        back[pl.ds(j, 1)] = turned.reshape(1, wa_n, rows_dev, cols_dev, width).astype(BF16)
        for q in range(wa_n):
            if q == 0:
                pl.when(j < ha_n - 1)(lambda: out2(j, 0).start())
            else:
                out2(j, q).start()
        return carry

    lax.fori_loop(0, ha_n, layer2, 0)
    out[pl.ds(me, 1)] = back[ha_n - 1, pl.ds(wa, 1)]
    for j in range(ha_n):
        for q in range(wa_n):
            if j < ha_n - 1 or q > 0:
                out2(j, q).wait()
    for c in range(chunks):
        for k in range(1, peers):
            out1(c, k).wait_send()


def fits(tokens, ha_n, wa_n):
    frames, rows_dev, cols_dev, _ = tokens.shape
    return (
        frames == ha_n * wa_n
        and rows_dev == 8
        and ROWS % (frames * rows_dev) == 0
        and cols_dev % (ROWS // (frames * rows_dev)) == 0
        and (frames * rows_dev * cols_dev) % ROWS == 0
        and ROWS % (rows_dev * cols_dev) == 0
        and cols_dev * wa_n * rows_dev == ROWS
        and wa_n * (ROWS // (frames * rows_dev)) * rows_dev * ha_n == ROWS
    )


def shards(*arrays):
    tokens, ng, wg, wc, ws, cv, cc, sb, rl, sk, og, wo = arrays
    ha_n, wa_n = lax.axis_size("ha"), lax.axis_size("wa")
    if not fits(tokens, ha_n, wa_n):
        return shards_general(*arrays)
    ws = ws.transpose(0, 2, 1)
    frames, rows_dev, cols_dev, width = tokens.shape
    count = frames * rows_dev * cols_dev
    layers, _, wide = wg.shape
    inner = wide // 2
    cpc = ROWS // (frames * rows_dev)
    chunks = cols_dev // cpc
    blocks = 4
    early = (frames, rows_dev * cols_dev)
    late = (cols_dev * wa_n, rows_dev * ha_n)
    vmem = pl.BlockSpec(memory_space=pltpu.VMEM)
    hbm = pl.BlockSpec(memory_space=pl.ANY)
    sizes = (ha_n, wa_n, frames, rows_dev, cols_dev, width)
    dma = pltpu.SemaphoreType.DMA
    return pl.pallas_call(
        functools.partial(sweeps, sizes),
        out_shape=jax.ShapeDtypeStruct(tokens.shape, BF16),
        in_specs=[hbm] * 12,
        out_specs=vmem,
        scratch_shapes=[
            pltpu.VMEM(tokens.shape, BF16),
            *(pltpu.VMEM(a.shape, a.dtype) for a in (ng, wg, wc, ws, cv, cc, sb, rl, sk, og, wo)),
            pltpu.VMEM(early + (width,), F32),
            pltpu.VMEM(late + (width,), F32),
            *(
                pltpu.VMEM((ROWS, size), F32)
                for size in (inner, inner, wc.shape[2], ws.shape[1], ws.shape[1])
            ),
            pltpu.VMEM((chunks, wa_n, cpc, ha_n, rows_dev, width), BF16),
            pltpu.VMEM((frames, chunks, cpc, rows_dev, width), BF16),
            pltpu.VMEM((ROWS, inner), F32),
            pltpu.VMEM((ROWS, inner), BF16),
            pltpu.VMEM((ha_n, wa_n, rows_dev, cols_dev, width), BF16),
            dma(()),
            dma((9,)),
            dma((layers, blocks)),
            dma((layers,)),
            dma((chunks, ha_n * wa_n)),
            dma((chunks, ha_n * wa_n)),
            dma((ha_n, wa_n)),
            dma((ha_n, wa_n)),
        ],
        compiler_params=pltpu.CompilerParams(
            collective_id=0, has_side_effects=True, vmem_limit_bytes=67043328
        ),
    )(tokens, ng, wg, wc, ws, cv, cc, sb, rl, sk, og, wo)


def solution(mesh):
    in_specs = (P("ba", "ha", "wa", None),) + (P(),) * 11
    out_specs = P("ba", "ha", "wa", None)
    return jax.shard_map(shards, mesh=mesh, in_specs=in_specs, out_specs=out_specs, check_vma=False)
```

```python
import functools
import jax
import jax.numpy as jnp
from jax import lax
from jax.experimental import pallas as pl
from jax.experimental.pallas import tpu as pltpu
from jax.sharding import PartitionSpec as P


def causal_conv(values, kernel):
    length = values.shape[1]
    taps = kernel.shape[0]
    padded = jnp.pad(values, ((0, 0), (taps - 1, 0), (0, 0)))
    total = jnp.zeros_like(values)
    for offset in range(taps):
        total = total + padded[:, offset : offset + length, :] * kernel[offset]
    return total


def mixer(stream, params):
    (
        norm_gain,
        w_gatevals,
        w_coupling,
        w_steps,
        conv_values,
        conv_coupling,
        step_bias,
        rate_log,
        skip_gain,
        out_gain,
        w_output,
    ) = params
    count, length, width = stream.shape
    inner = w_gatevals.shape[1] // 2
    states = w_coupling.shape[1] // 2
    heads = w_steps.shape[1]
    headdim = inner // heads
    flat = stream.reshape(count * length, width).astype(jnp.float32)
    normed = (
        flat * lax.rsqrt(jnp.mean(flat * flat, axis=-1, keepdims=True) + 1e-05) * norm_gain
    ).astype(jnp.bfloat16)
    gatevals = jnp.dot(normed, w_gatevals, preferred_element_type=jnp.float32).astype(jnp.bfloat16)
    coupling = jnp.dot(normed, w_coupling, preferred_element_type=jnp.float32).astype(jnp.bfloat16)
    step_raw = jnp.dot(normed, w_steps, preferred_element_type=jnp.float32)
    gate = gatevals[:, :inner]
    values = gatevals[:, inner:]
    xs = jax.nn.silu(
        causal_conv(values.astype(jnp.float32).reshape(count, length, inner), conv_values)
    ).astype(jnp.bfloat16)
    maps = jax.nn.silu(
        causal_conv(coupling.astype(jnp.float32).reshape(count, length, 2 * states), conv_coupling)
    ).astype(jnp.bfloat16)
    input_map = maps[:, :, :states]
    output_map = maps[:, :, states:]
    steps = jax.nn.softplus(step_raw.reshape(count, length, heads) + step_bias)
    cumul = jnp.cumsum(steps * -jnp.exp(rate_log), axis=1).transpose(0, 2, 1)
    steps_heads = steps.transpose(0, 2, 1)
    positions = jnp.arange(length, dtype=jnp.int32)
    lower = positions[:, None] >= positions[None, :]
    spread = cumul[:, :, :, None] - cumul[:, :, None, :]
    decay = jnp.exp(jnp.where(lower[None, None, :, :], spread, -jnp.inf))
    scores = jnp.einsum("ntk,nsk->nts", output_map, input_map, preferred_element_type=jnp.float32)
    weights = (scores[:, None, :, :] * decay * steps_heads[:, :, None, :]).astype(jnp.bfloat16)
    heads_in = xs.reshape(count, length, heads, headdim)
    mixed = jnp.einsum("nhts,nshp->nthp", weights, heads_in, preferred_element_type=jnp.float32)
    mixed = mixed + skip_gain[:, None] * heads_in.astype(jnp.float32)
    gated = mixed.reshape(count * length, inner) * jax.nn.silu(gate.astype(jnp.float32))
    normal = (
        gated * lax.rsqrt(jnp.mean(gated * gated, axis=-1, keepdims=True) + 1e-05) * out_gain
    ).astype(jnp.bfloat16)
    update = jnp.dot(normal, w_output, preferred_element_type=jnp.float32)
    return (flat + update).astype(jnp.bfloat16).reshape(count, length, width)


def shards_general(
    tokens,
    norm_gain,
    w_gatevals,
    w_coupling,
    w_steps,
    conv_values,
    conv_coupling,
    step_bias,
    rate_log,
    skip_gain,
    out_gain,
    w_output,
):
    stacked = (
        norm_gain,
        w_gatevals,
        w_coupling,
        w_steps,
        conv_values,
        conv_coupling,
        step_bias,
        rate_log,
        skip_gain,
        out_gain,
        w_output,
    )

    def params_of(index):
        return tuple((member[index] for member in stacked))

    frames, rows_dev, cols_dev, width = tokens.shape
    height_devs = lax.axis_size("ha")
    width_devs = lax.axis_size("wa")
    streams = tokens.transpose(1, 2, 0, 3).reshape(rows_dev * cols_dev, frames, width)
    current = (
        mixer(streams, params_of(0))
        .reshape(rows_dev, cols_dev, frames, width)
        .transpose(2, 0, 1, 3)
    )
    piece = lax.all_to_all(current, "ha", split_axis=0, concat_axis=1, tiled=True)
    frame_part, rows_all, col_count, _ = piece.shape
    streams = piece.transpose(0, 2, 1, 3).reshape(frame_part * col_count, rows_all, width)
    output = mixer(streams, params_of(1))
    current = output.reshape(frame_part, col_count, rows_all, width).transpose(0, 2, 1, 3)
    frame_part = current.shape[0]
    rows_all = current.shape[1]
    split_rows = current.reshape(frame_part, rows_all // width_devs, width_devs, cols_dev, width)
    piece = lax.all_to_all(split_rows, "wa", split_axis=2, concat_axis=3, tiled=True)
    part_frames, row_count, single, cols_all, _ = piece.shape
    streams = piece.reshape(part_frames * row_count * single, cols_all, width)
    output = mixer(streams, params_of(2))
    current = output.reshape(part_frames, row_count, single, cols_all, width)
    row_group = rows_dev // width_devs
    arranged = current.reshape(frame_part, height_devs, row_group, width_devs, cols_dev, width)
    arranged = arranged.transpose(1, 3, 0, 2, 4, 5).reshape(
        height_devs * width_devs, frame_part, row_group, cols_dev, width
    )
    received = lax.all_to_all(arranged, ("ha", "wa"), split_axis=0, concat_axis=0, tiled=True)
    received = received.reshape(height_devs, width_devs, frame_part, row_group, cols_dev, width)
    result = received.transpose(0, 2, 3, 1, 4, 5).reshape(frames, rows_dev, cols_dev, width)
    return result


ROWS = 128
F32 = jnp.float32
BF16 = jnp.bfloat16
MESH = pl.DeviceIdType.MESH


LOG2E = 1.4426950408889634


def silu_of_half(half):
    return half + half * jnp.tanh(half)


def rounded(x):
    return x.astype(BF16).astype(F32)


def project(layer, length, stride, x, refs, n_block, emit, wait=None):
    wg, wc, ws, ng, cv, cc, sb, rl = refs
    rows = x.shape[0]
    inner = cv.shape[2]
    taps = cv.shape[1]

    def shift(v, by):
        if stride == 1:
            position = lax.broadcasted_iota(jnp.int32, v.shape, 0) % length
            return jnp.where(position >= by, pltpu.roll(v, by, 0), 0.0)
        pad = jnp.zeros((by * stride, v.shape[1]), v.dtype)
        return jnp.concatenate([pad, v[: rows - by * stride]], axis=0)

    def conv(v, kernel):
        half = 0.5 * kernel
        total = v * half[taps - 1 : taps]
        for back in range(1, taps):
            total = total + shift(v, back) * half[taps - 1 - back : taps - back]
        return rounded(silu_of_half(total))

    scale = lax.rsqrt(jnp.mean(x * x, axis=-1, keepdims=True) + 1e-05)
    normed = (x * scale * ng[layer : layer + 1, :]).astype(BF16)
    coupling = rounded(jnp.dot(normed, wc[layer], preferred_element_type=F32))
    emit("maps", 0, conv(coupling, cc[layer]))
    raw = lax.dot_general(normed, ws[layer], (((1,), (1,)), ((), ())), preferred_element_type=F32)
    raw = raw + sb[layer : layer + 1, :]
    steps = jnp.maximum(raw, 0.0) + jnp.log1p(jnp.exp(-jnp.abs(raw)))
    cumul = steps * -jnp.exp(rl[layer : layer + 1, :])
    by = 1
    while by < length:
        cumul = cumul + shift(cumul, by)
        by *= 2
    cumul = cumul * LOG2E
    emit("decay", 0, cumul)
    emit("source", 0, cumul - jnp.log(steps) * LOG2E)
    for first in range(0, 2 * inner, n_block):
        if wait is not None:
            wait(first)
        block = rounded(
            jnp.dot(normed, wg[layer, :, first : first + n_block], preferred_element_type=F32)
        )
        if first < inner:
            emit("gate", first, silu_of_half(0.5 * block))
        else:
            at = first - inner
            emit("xs", at, conv(block, cv[layer, :, at : at + n_block]))


def mix(layer, length, stride, read, x, params, gated, normal):
    sk, og, wo = params
    maps, decay_to, source = read("maps"), read("decay"), read("source")
    rows, heads = decay_to.shape
    inner = og.shape[1]
    headdim = inner // heads
    states = maps.shape[1] // 2
    i = lax.broadcasted_iota(jnp.int32, (rows, rows), 0)
    j = lax.broadcasted_iota(jnp.int32, (rows, rows), 1)
    if stride == 1:
        same = (i // length) == (j // length)
    else:
        same = (i % stride) == (j % stride)
    mask = same & (i >= j)
    maps = maps.astype(BF16)
    scores = lax.dot_general(
        maps[:, states:], maps[:, :states], (((1,), (1,)), ((), ())), preferred_element_type=F32
    )
    source_t = source.T
    pair = 2 * headdim
    lane = lax.broadcasted_iota(jnp.int32, (1, pair), 1)
    squares = jnp.zeros((rows, pair), F32)
    for p in range(heads // 2):
        lanes = slice(p * pair, (p + 1) * pair)
        xs = read("xs", lanes)
        weights = []
        for h in (2 * p, 2 * p + 1):
            spread = decay_to[:, h : h + 1] - source_t[h : h + 1, :]
            decay = jnp.exp2(jnp.where(mask, spread, -jnp.inf))
            weights.append((scores * decay).astype(BF16))
        both = jnp.concatenate(
            [jnp.where(lane < headdim, xs, 0.0), jnp.where(lane < headdim, 0.0, xs)], axis=0
        ).astype(BF16)
        mixed = jnp.dot(jnp.concatenate(weights, axis=1), both, preferred_element_type=F32)
        skip = jnp.where(
            lane < headdim,
            sk[layer : layer + 1, 2 * p : 2 * p + 1],
            sk[layer : layer + 1, 2 * p + 1 : 2 * p + 2],
        )
        part = (mixed + skip * xs) * read("gate", lanes)
        squares = squares + part * part
        gated[:, lanes] = part
    scale = lax.rsqrt(jnp.sum(squares, axis=-1, keepdims=True) / inner + 1e-05)
    for p in range(heads // 2):
        lanes = slice(p * pair, (p + 1) * pair)
        normal[:, lanes] = (gated[:, lanes] * scale * og[layer : layer + 1, lanes]).astype(BF16)
    return x + jnp.dot(normal[...], wo[layer], preferred_element_type=F32)


def swap_matrix(outer, first, second):
    n = outer * first * second
    i = lax.broadcasted_iota(jnp.int32, (n, n), 0)
    j = lax.broadcasted_iota(jnp.int32, (n, n), 1)
    o, a, b = i // (first * second), (i // second) % first, i % second
    return jnp.where(o * first * second + b * first + a == j, 1.0, 0.0).astype(BF16)


def sweeps(
    sizes, tok_hbm, ng_hbm, wg_hbm, wc_hbm, ws_hbm, cv_hbm, cc_hbm, sb_hbm, rl_hbm, sk_hbm,
    og_hbm, wo_hbm, out, tok, ng, wg, wc, ws, cv, cc, sb, rl, sk, og, wo, x0, x2,
    gate, xs, maps, decay, source,
    landed, sent, gated, normal, back,
    tok_sem, small_sem, wg_sem, wo_sem, send1, recv1, send2, recv2,
):
    ha_n, wa_n, frames, rows_dev, cols_dev, width = sizes
    peers = ha_n * wa_n
    cpc = ROWS // (frames * rows_dev)
    chunks = cols_dev // cpc
    rows_all, cols_all = rows_dev * ha_n, cols_dev * wa_n
    tokens = frames * rows_dev * cols_dev
    ha, wa = lax.axis_index("ha"), lax.axis_index("wa")
    me = ha * wa_n + wa
    blocks = wg_sem.shape[1]
    n_block = wg.shape[2] // blocks
    n_dot = n_block // 2

    def device(index):
        return {"ha": index // wa_n, "wa": lax.rem(index, wa_n)}

    fetch = pltpu.make_async_copy(tok_hbm, tok, tok_sem)
    fetch.start()
    small = []
    for n, (src, dst) in enumerate(
        (
            (ng_hbm, ng), (wc_hbm, wc), (ws_hbm, ws), (cv_hbm, cv), (cc_hbm, cc),
            (sb_hbm, sb), (rl_hbm, rl), (sk_hbm, sk), (og_hbm, og),
        )
    ):
        copy = pltpu.make_async_copy(src, dst, small_sem.at[n])
        copy.start()
        small.append(copy)
    wg_copies = {}
    wo_copies = []
    layers = wg.shape[0]

    def start_weights(layer):
        for b in range(blocks):
            span = pl.ds(b * n_block, n_block)
            copy = pltpu.make_async_copy(
                wg_hbm.at[layer, :, span], wg.at[layer, :, span], wg_sem.at[layer, b]
            )
            copy.start()
            wg_copies[layer, b] = copy
        copy = pltpu.make_async_copy(wo_hbm.at[layer], wo.at[layer], wo_sem.at[layer])
        copy.start()
        wo_copies.append(copy)

    start_weights(0)

    barrier = pltpu.get_barrier_semaphore()
    for k in range(1, peers):
        pl.semaphore_signal(
            barrier, inc=1, device_id=device(lax.rem(me + k, peers)), device_id_type=MESH
        )

    refs = (wg, wc, ws, ng, cv, cc, sb, rl)
    params = (sk, og, wo)
    kept = dict(gate=gate, xs=xs, maps=maps, decay=decay, source=source)

    def emit(name, first, value):
        kept[name][:, first : first + value.shape[1]] = value

    def read(name, lanes=slice(None)):
        return kept[name][:, lanes]

    def run(layer, length, stride, x):
        project(layer, length, stride, x, refs, n_dot, emit)
        return mix(layer, length, stride, read, x, params, gated, normal)

    fetch.wait()
    for copy in small:
        copy.wait()
    swap = swap_matrix(ROWS // (rows_dev * cols_dev), cols_dev, rows_dev)
    for first in range(0, tokens, ROWS):
        part = tok[...].astype(F32).reshape(tokens, width)[first : first + ROWS].astype(BF16)
        group = ROWS // (rows_dev * cols_dev)
        x0[first // ROWS * group : (first // ROWS + 1) * group] = jnp.dot(
            swap, part, preferred_element_type=F32
        ).reshape(group, rows_dev * cols_dev, width)

    for b in range(blocks):
        wg_copies[0, b].wait()
    wo_copies[0].wait()
    for layer in range(1, layers):
        start_weights(layer)
    pl.semaphore_wait(barrier, peers - 1)

    span = rows_dev * cpc

    def view(ref, c, size):
        return ref[:, pl.ds(pl.multiple_of(c * size, size), size), :].reshape(ROWS, width)

    def out1(c, k):
        peer = lax.rem(me + k, peers)
        return pltpu.make_async_remote_copy(
            src_ref=sent.at[peer, c],
            dst_ref=landed.at[c, wa, :, ha],
            send_sem=send1.at[c, k],
            recv_sem=recv1.at[c, k],
            device_id=device(peer),
            device_id_type=MESH,
        )

    def layer0(c, carry):
        y = run(0, frames, span, view(x0, c, span))
        sent[:, pl.ds(c, 1)] = y.reshape(frames, 1, cpc, rows_dev, width).astype(BF16)
        for k in range(1, peers):
            out1(c, k).start()
        landed[pl.ds(c, 1), pl.ds(wa, 1), :, pl.ds(ha, 1)] = sent[
            pl.ds(me, 1), pl.ds(c, 1)
        ].reshape(1, 1, cpc, 1, rows_dev, width)
        return carry

    lax.fori_loop(0, chunks, layer0, 0)

    for b in range(blocks):
        wg_copies[1, b].wait()
    wo_copies[1].wait()

    def layer1(c, carry):
        for k in range(1, peers):
            out1(c, k).wait_recv()
        y = run(1, rows_all, 1, landed[pl.ds(c, 1)].astype(F32).reshape(ROWS, width))
        y = rounded(y).reshape(wa_n, cpc, rows_all, width)
        for w in range(wa_n):
            x2[pl.ds(w * cols_dev + c * cpc, cpc)] = y[w]
        return carry

    lax.fori_loop(0, chunks, layer1, 0)

    for b in range(blocks):
        wg_copies[2, b].wait()
    wo_copies[2].wait()
    swap2 = swap_matrix(wa_n, rows_dev, cols_dev)

    def target(j):
        if ha_n != 4:
            return lax.rem(ha + j + 1, ha_n)
        mirrored = ha + ((j + 1) // 2 % 2) * (ha_n - 1 - 2 * ha)
        return lax.rem(mirrored + (1 - j % 2) * (ha_n // 2), ha_n)

    def out2(j, q):
        peer_ha, peer_wa = target(j), lax.rem(wa + q, wa_n)
        return pltpu.make_async_remote_copy(
            src_ref=back.at[j, peer_wa],
            dst_ref=out.at[me],
            send_sem=send2.at[j, q],
            recv_sem=recv2.at[j, q],
            device_id={"ha": peer_ha, "wa": peer_wa},
            device_id_type=MESH,
        )

    def layer2(j, carry):
        c = target(j)
        y = run(2, cols_all, rows_dev, view(x2, c, rows_dev))
        turned = jnp.dot(swap2, y.astype(BF16), preferred_element_type=F32)
        back[pl.ds(j, 1)] = turned.reshape(1, wa_n, rows_dev, cols_dev, width).astype(BF16)
        for q in range(wa_n):
            if q == 0:
                pl.when(j < ha_n - 1)(lambda: out2(j, 0).start())
            else:
                out2(j, q).start()
        return carry

    lax.fori_loop(0, ha_n, layer2, 0)
    out[pl.ds(me, 1)] = back[ha_n - 1, pl.ds(wa, 1)]
    for j in range(ha_n):
        for q in range(wa_n):
            if j < ha_n - 1 or q > 0:
                out2(j, q).wait()
    for c in range(chunks):
        for k in range(1, peers):
            out1(c, k).wait_send()


def hand_on(src, dst):
    dst[...] = src[...]


def fits(tokens, ha_n, wa_n):
    frames, rows_dev, cols_dev, _ = tokens.shape
    return (
        frames == ha_n * wa_n
        and frames % 2 == 0
        and rows_dev == 8
        and ROWS % (frames * rows_dev) == 0
        and cols_dev % (ROWS // (frames * rows_dev)) == 0
        and (frames * rows_dev * cols_dev) % ROWS == 0
        and ROWS % (rows_dev * cols_dev) == 0
        and cols_dev * wa_n * rows_dev == ROWS
        and wa_n * (ROWS // (frames * rows_dev)) * rows_dev * ha_n == ROWS
    )


def shards(*arrays):
    tokens, ng, wg, wc, ws, cv, cc, sb, rl, sk, og, wo = arrays
    ha_n, wa_n = lax.axis_size("ha"), lax.axis_size("wa")
    if not fits(tokens, ha_n, wa_n):
        return shards_general(*arrays)
    ws = ws.transpose(0, 2, 1)
    frames, rows_dev, cols_dev, width = tokens.shape
    count = frames * rows_dev * cols_dev
    layers, _, wide = wg.shape
    inner = wide // 2
    cpc = ROWS // (frames * rows_dev)
    chunks = cols_dev // cpc
    blocks = 4
    early = (frames, rows_dev * cols_dev)
    late = (cols_dev * wa_n, rows_dev * ha_n)
    vmem = pl.BlockSpec(memory_space=pltpu.VMEM)
    hbm = pl.BlockSpec(memory_space=pl.ANY)
    sizes = (ha_n, wa_n, frames, rows_dev, cols_dev, width)
    dma = pltpu.SemaphoreType.DMA
    result = pl.pallas_call(
        functools.partial(sweeps, sizes),
        out_shape=jax.ShapeDtypeStruct(tokens.shape, BF16),
        in_specs=[hbm] * 12,
        out_specs=vmem,
        scratch_shapes=[
            pltpu.VMEM(tokens.shape, BF16),
            *(pltpu.VMEM(a.shape, a.dtype) for a in (ng, wg, wc, ws, cv, cc, sb, rl, sk, og, wo)),
            pltpu.VMEM(early + (width,), F32),
            pltpu.VMEM(late + (width,), F32),
            *(
                pltpu.VMEM((ROWS, size), F32)
                for size in (inner, inner, wc.shape[2], ws.shape[1], ws.shape[1])
            ),
            pltpu.VMEM((chunks, wa_n, cpc, ha_n, rows_dev, width), BF16),
            pltpu.VMEM((frames, chunks, cpc, rows_dev, width), BF16),
            pltpu.VMEM((ROWS, inner), F32),
            pltpu.VMEM((ROWS, inner), BF16),
            pltpu.VMEM((ha_n, wa_n, rows_dev, cols_dev, width), BF16),
            dma(()),
            dma((9,)),
            dma((layers, blocks)),
            dma((layers,)),
            dma((chunks, ha_n * wa_n)),
            dma((chunks, ha_n * wa_n)),
            dma((ha_n, wa_n)),
            dma((ha_n, wa_n)),
        ],
        compiler_params=pltpu.CompilerParams(
            collective_id=0, has_side_effects=True, vmem_limit_bytes=67043328
        ),
    )(tokens, ng, wg, wc, ws, cv, cc, sb, rl, sk, og, wo)
    half = (frames // 2,) + tokens.shape[1:]
    block = pl.BlockSpec(half, lambda i: (i, 0, 0, 0))
    return pl.pallas_call(
        hand_on,
        out_shape=jax.ShapeDtypeStruct(tokens.shape, BF16),
        grid=(2,),
        in_specs=[block],
        out_specs=block,
    )(result)


def solution(mesh):
    in_specs = (P("ba", "ha", "wa", None),) + (P(),) * 11
    out_specs = P("ba", "ha", "wa", None)
    return jax.shard_map(shards, mesh=mesh, in_specs=in_specs, out_specs=out_specs, check_vma=False)
```
